512 devices in a mesh: patch: 32 (over z, core), line: 16 (over y, x).
Axes of the slice: x: 4, y: 4, z: 16, core: 2. Of those that a mesh axis runs over, the one named last changes fastest.
Arguments:
- residual: float32 [128, 80, 2, 4096], P('line', None, None, 'patch'), may hold values from -6 to 6
- forward_maps: float32 [32, 128, 6400], P('patch', 'line'), as said below
- pivot_inverse: float32 [32, 128, 6400], P('patch', 'line'), as said below
- backward_maps: float32 [32, 128, 6400], P('patch', 'line'), as said below
- face_flux: float32 [32, 128, 4, 6400], P('patch', 'line'), as said below
- mass_scale: float32 [128, 4096], P('line', 'patch'), may hold values from 0.2 to 1
- frequencies: float32 [2], replicated, may hold values from 0.25 to 1
- line_order: int32 [4096], P('patch'), may hold values from 0 to 127, as said below
Outputs:
- update: float32 [128, 80, 2, 4096], P('line', None, None, 'patch')
- next_residual: float32 [128, 80, 2, 4096], P('line', None, None, 'patch')
The draws below stay inside these ranges and needn't reach their ends.
Inputs may be any that keep to these rules, and one draw needn't show every extreme that they name: `line_order`: for each patch, its 128 entries are a permutation of 0 to 127. `forward_maps`: each block, read row by row, is the real form [[a, -b], [b, a]] of a complex block a + i b. `pivot_inverse`: each block, read row by row, is the real form [[a, -b], [b, a]] of a complex block a + i b. `backward_maps`: each block, read row by row, is the real form [[a, -b], [b, a]] of a complex block a + i b. `face_flux`: each block, read row by row, is the real form [[a, -b], [b, a]] of a complex block a + i b.
All inputs are finite; a program needn't handle non-finite values.
Results may differ from the reference program's by a relative error of at most 0.00012.
Values sent between devices are 32-bit elements; how exact they have to be, the bound alone decides.
A program may use at most 64 MiB of HBM per device.

```python
import math
import jax
import jax.numpy as jnp
from jax import lax

BLOCK = 40
FREQ = 2
LINE_ELEMENTS = 128
SX = 32
SY = 4
SWEEPS = 2
LINES_DEV = 128
WALL_PATCHES = 32
LINES = 4096


SPREAD = 0.25


def assemble(real_part, imag_part):
    top_rows = jnp.concatenate([real_part, -imag_part], axis=-1)
    bottom_rows = jnp.concatenate([imag_part, real_part], axis=-1)
    joined = jnp.concatenate([top_rows, bottom_rows], axis=-2)
    return joined.reshape(joined.shape[:-2] + (4 * BLOCK * BLOCK,))


def chain_blocks(key, salt):
    random_subkeys = jax.random.split(jax.random.fold_in(key, salt), 7)
    slow_share = 0.5
    slow_mask = jax.random.uniform(random_subkeys[0], (WALL_PATCHES, 1, BLOCK)) < slow_share
    slow_rate = jax.random.uniform(random_subkeys[1], (WALL_PATCHES, 1, BLOCK), minval=0.5, maxval=1.5)
    fast_rate = jax.random.uniform(random_subkeys[2], (WALL_PATCHES, 1, BLOCK), minval=2.5, maxval=5.0)
    slow_diagonal = jnp.sqrt(jnp.exp(-2.0 * slow_rate / LINE_ELEMENTS) - SPREAD * SPREAD * slow_share)
    fast_diagonal = jnp.exp(-fast_rate / 40.0)
    diagonal = jnp.where(slow_mask, slow_diagonal, fast_diagonal) * jnp.ones((WALL_PATCHES, LINE_ELEMENTS, BLOCK), jnp.float32)
    positions_list = jax.random.randint(random_subkeys[3], (WALL_PATCHES, 3), 0, LINE_ELEMENTS)
    surge_mask = jnp.any(jnp.arange(LINE_ELEMENTS)[None, :, None] == positions_list[:, None, :], axis=-1)
    surge_removal = jax.random.uniform(random_subkeys[4], (WALL_PATCHES, LINE_ELEMENTS), minval=0.5, maxval=0.8)
    scaling_factor = jnp.where(surge_mask, surge_removal, 1.0)
    scale = SPREAD / math.sqrt(2 * BLOCK)
    real_part = jax.random.normal(random_subkeys[5], (WALL_PATCHES, LINE_ELEMENTS, BLOCK, BLOCK)) * scale
    real_part = real_part + diagonal[..., None] * jnp.eye(BLOCK, dtype=jnp.float32)
    imag_part = jax.random.normal(random_subkeys[6], (WALL_PATCHES, LINE_ELEMENTS, BLOCK, BLOCK)) * scale
    return (assemble(real_part, imag_part) * scaling_factor[:, :, None]).astype(jnp.float32)


def draw_forward_maps(key, part):
    return chain_blocks(key, 11)


def draw_backward_maps(key, part):
    return chain_blocks(key, 23)


def draw_pivot_inverse(key, part):
    random_subkeys = jax.random.split(jax.random.fold_in(key, 37), 3)
    lowest = 0.5
    highest = 2.0
    diagonal = jnp.exp(jax.random.uniform(random_subkeys[0], (WALL_PATCHES, LINE_ELEMENTS, BLOCK), minval=math.log(lowest), maxval=math.log(highest)))
    scale = 0.3 / math.sqrt(2 * BLOCK)
    real_part = jax.random.normal(random_subkeys[1], (WALL_PATCHES, LINE_ELEMENTS, BLOCK, BLOCK)) * scale
    real_part = real_part + diagonal[..., None] * jnp.eye(BLOCK, dtype=jnp.float32)
    imag_part = jax.random.normal(random_subkeys[2], (WALL_PATCHES, LINE_ELEMENTS, BLOCK, BLOCK)) * scale
    return assemble(real_part, imag_part).astype(jnp.float32)


def draw_face_flux(key, part):
    random_subkeys = jax.random.split(jax.random.fold_in(key, 41), 3)
    scale = 0.25 / math.sqrt(2 * BLOCK)
    diagonal = jax.random.uniform(random_subkeys[0], (WALL_PATCHES, LINE_ELEMENTS, 4, BLOCK), minval=0.05, maxval=0.2)
    real_part = jax.random.normal(random_subkeys[1], (WALL_PATCHES, LINE_ELEMENTS, 4, BLOCK, BLOCK)) * scale
    real_part = real_part + diagonal[..., None] * jnp.eye(BLOCK, dtype=jnp.float32)
    imag_part = jax.random.normal(random_subkeys[2], (WALL_PATCHES, LINE_ELEMENTS, 4, BLOCK, BLOCK)) * scale
    return assemble(real_part, imag_part).astype(jnp.float32)


def shuffle_patch(subkey):
    return jax.random.permutation(subkey, LINES_DEV)


def draw_line_order(key, part):
    random_subkeys = jax.random.split(jax.random.fold_in(key, 5), WALL_PATCHES)
    shuffled = jax.vmap(shuffle_patch)(random_subkeys)
    return shuffled.reshape(LINES).astype(jnp.int32)


def block_scale(rng, dims, cuts, smallest, top_value):
    loudness = 1.0
    for position, shards_of in cuts:
        steps = jax.random.uniform(jax.random.fold_in(jax.random.fold_in(rng, 6), position), (shards_of,), jnp.float32, smallest / len(cuts), top_value / len(cuts))
        loudness = loudness * jnp.repeat(jnp.exp(steps), dims[position] // shards_of).reshape((-1,) + (1,) * (len(dims) - 1 - position))
    return loudness


def noise(key, extent, scale, bound, cuts=(), held_as=jnp.bfloat16):
    gain = block_scale(key, extent, cuts, -0.22, 0.18) if cuts else 1.0
    entries = jax.random.normal(key, extent, jnp.float32) * scale * gain
    return jnp.minimum(jnp.maximum(entries, -bound), bound).astype(held_as)


def setup_inputs(seed: int = 0) -> dict:
    seeds = jax.random.split(jax.random.key(seed), 9)
    residual = noise(seeds[0], (LINE_ELEMENTS, 2 * BLOCK, FREQ, LINES), 1.0, 6.0, ((0, 16), (3, 32)), jnp.float32)
    forward_maps = draw_forward_maps(jax.random.fold_in(seeds[8], 71), 0)
    pivot_inverse = draw_pivot_inverse(jax.random.fold_in(seeds[8], 71), 0)
    backward_maps = draw_backward_maps(jax.random.fold_in(seeds[8], 71), 0)
    face_flux = draw_face_flux(jax.random.fold_in(seeds[8], 71), 0)
    mass_scale = jnp.clip(jnp.exp(math.log(1.0) - 1.609438 * jax.random.uniform(seeds[5], (LINE_ELEMENTS, LINES), jnp.float32) ** block_scale(seeds[5], (LINE_ELEMENTS, LINES), ((0, 16), (1, 32)), -0.2, 0.2)), 0.2, 1.0)
    frequencies = jnp.clip(jnp.exp(jax.random.uniform(seeds[6], (FREQ,), jnp.float32, math.log(0.25), math.log(1.0))), 0.25, 1.0)
    line_order = draw_line_order(jax.random.fold_in(seeds[8], 71), 0)
    return dict(residual=residual, forward_maps=forward_maps, pivot_inverse=pivot_inverse, backward_maps=backward_maps, face_flux=face_flux, mass_scale=mass_scale, frequencies=frequencies, line_order=line_order)


precise = lax.Precision.HIGHEST
RELAXATION = 0.8


def reference(residual, forward_maps, pivot_inverse, backward_maps, face_flux, mass_scale, frequencies, line_order):
    lane_count = SX * SY
    width = 2 * BLOCK
    ordering = line_order.reshape(WALL_PATCHES, lane_count)
    onehot = (ordering[:, :, None] == jnp.arange(lane_count, dtype=jnp.int32)[None, None, :]).astype(jnp.float32)

    def to_grid(values):
        shaped = values.reshape(values.shape[:-1] + (WALL_PATCHES, lane_count))
        return jnp.einsum('...ps,psc->...pc', shaped, onehot, precision=precise)

    def to_store(values):
        stored = jnp.einsum('...pc,psc->...ps', values, onehot, precision=precise)
        return stored.reshape(values.shape[:-2] + (LINES,))

    forward = jnp.transpose(forward_maps.reshape(WALL_PATCHES, LINE_ELEMENTS, width, width), (1, 0, 2, 3))
    pivots = jnp.transpose(pivot_inverse.reshape(WALL_PATCHES, LINE_ELEMENTS, width, width), (1, 0, 2, 3))
    backward = jnp.transpose(backward_maps.reshape(WALL_PATCHES, LINE_ELEMENTS, width, width), (1, 0, 2, 3))
    fluxes = jnp.transpose(face_flux.reshape(WALL_PATCHES, LINE_ELEMENTS, 4, width, width), (1, 2, 0, 3, 4))

    def apply_blocks(blocks, state_now):
        return jnp.einsum('pij,jfpl->ifpl', blocks, state_now, precision=precise)

    def line_solve(current):
        start_state = jnp.zeros(current.shape[1:], jnp.float32)

        def down(carried, inputs):
            blocks, pieces = inputs
            carried = pieces + apply_blocks(blocks, carried)
            return carried, carried

        _, forward_sweep = lax.scan(down, start_state, (forward, current))
        scaled = jnp.einsum('kpij,kjfpl->kifpl', pivots, forward_sweep, precision=precise)

        def climb(carried, inputs):
            blocks, pieces = inputs
            carried = pieces - apply_blocks(blocks, carried)
            return carried, carried

        _, solved = lax.scan(climb, start_state, (backward, scaled), reverse=True)
        return solved

    def lateral(values):
        grid_view = values.reshape(values.shape[:3] + (WALL_PATCHES * SY, SX))
        upstream = jnp.pad(grid_view[..., :-1], ((0, 0),) * 4 + ((1, 0),))
        downstream = jnp.pad(grid_view[..., 1:], ((0, 0),) * 4 + ((0, 1),))
        spanwise_low = jnp.roll(grid_view, 1, axis=3)
        spanwise_high = jnp.roll(grid_view, -1, axis=3)
        summed = jnp.zeros(values.shape, jnp.float32)
        for direction, neighbor in enumerate((upstream, downstream, spanwise_low, spanwise_high)):
            neighbor = neighbor.reshape(values.shape)
            summed = summed + jnp.einsum('kpij,kjfpl->kifpl', fluxes[:, direction], neighbor, precision=precise)
        return summed

    mass_grid = to_grid(mass_scale)

    def rotate_phase(values):
        turned = jnp.concatenate([-values[:, BLOCK:], values[:, :BLOCK]], axis=1)
        return frequencies[None, None, :, None, None] * mass_grid[:, None, None, :, :] * turned

    current = to_grid(residual)
    update = jnp.zeros(current.shape, jnp.float32)
    for repeat in range(SWEEPS):
        correction = line_solve(current)
        update = update + RELAXATION * correction
        current = (1.0 - RELAXATION) * current - RELAXATION * (rotate_phase(correction) + lateral(correction))
    return to_store(update), to_store(current)
```

```python
import functools

import jax
import jax.numpy as jnp
from jax import lax
from jax.experimental import pallas as pl
from jax.experimental.pallas import tpu as pltpu
from jax.sharding import PartitionSpec as P

SX = 32
RELAXATION = 0.8
KEEP = 1.0 - RELAXATION
C = 40
W = 80
K = 8
L = 128
SIDE = 4
F32 = jnp.float32
BF16 = jnp.bfloat16
MESH = pl.DeviceIdType.MESH


def lanes(rows, width=L):
    return lax.broadcasted_iota(jnp.int32, (rows, width), 1)


def roll(x, by):
    by = by % L
    return x if by == 0 else pltpu.roll(x, by, 1)


def two(x):
    high = x.astype(BF16)
    return high, (x - high.astype(F32)).astype(BF16)


def rhs_of(x):
    high, low = two(x)
    return jnp.concatenate([high, low, high, jnp.zeros((16, x.shape[1]), BF16)], axis=0)


def lhs_of(w):
    lane = lanes(w.shape[0])
    high = w.astype(BF16).astype(F32)
    low = w - high
    moved = roll(high, W)
    first = jnp.where(lane < W, high, moved)
    second = jnp.where(lane < 32, moved, roll(low, 32))
    return jnp.concatenate([first, second], axis=1).astype(BF16)


def real_form(tile, at):
    lane = lanes(W)
    plain = roll(tile, -at)
    moved = roll(tile, C - at)
    turned = jnp.concatenate([-moved[C:], moved[:C]], axis=0)
    return jnp.where(lane < C, plain, jnp.where(lane < W, turned, 0.0))


def whole_map(top):
    lane = lanes(C)
    top = jnp.where(lane < W, top, 0.0)
    bottom = jnp.where(lane < C, -roll(top, -C), jnp.where(lane < W, roll(top, C), 0.0))
    return jnp.concatenate([top, bottom], axis=0)


def mm(a, b):
    return jnp.dot(a, b, preferred_element_type=F32)


def band(x, lo, hi):
    lane = lanes(x.shape[0])
    return jnp.where((lane >= lo) & (lane < hi), x, 0.0)


def eye_at(at):
    row = lax.broadcasted_iota(jnp.int32, (W, L), 0)
    return jnp.where(lanes(W) == row + at, jnp.where(row < C, 1.0, 0.0), 0.0)


def unfold(load, store, rows):
    lane = lanes(rows)
    for group in range(5):
        parts = [load(5 * group + q) for q in range(5)]
        for r in range(8):
            q, off = divmod(W * r, L)
            piece = roll(parts[q], -off)
            if off + W > L:
                piece = jnp.where(lane < L - off, piece, roll(parts[q + 1], -off))
            store(8 * group + r, piece)


def kernel(
    res, fwd, piv, bwd, flux, mass, freq, order,
    upd_out, res_out,
    tops, xtops, fd, bn, fx, qh, rp, dp, cp,
    st, zz, yl, ym, upd, ph, heads,
    sx, rx, sxm, rxm, sy, ry, sym, rym, sz, rz, ww, cw,
    sl, sh, hl, hh,
    send_x, recv_x, send_xm, recv_xm, send_y, recv_y, send_ym, recv_ym,
    send_z, recv_z, send_l, recv_l, send_h, recv_h,
):
    patch = lax.axis_index("patch")
    line = lax.axis_index("line")
    patches = lax.axis_size("patch")
    my_y, my_x = line // SIDE, line % SIDE
    before = lax.rem(patch + patches - 1, patches)
    after = lax.rem(patch + 1, patches)

    def in_row(d):
        return lax.rem(my_x + d, SIDE)

    def in_column(d):
        return lax.rem(my_y + d, SIDE)

    def row_peer(d):
        return (patch, my_y * SIDE + in_row(d))

    def column_peer(d):
        return (patch, in_column(d) * SIDE + my_x)

    barrier = pltpu.get_barrier_semaphore()
    for d in range(1, SIDE):
        pl.semaphore_signal(barrier, inc=1, device_id=row_peer(d), device_id_type=MESH)
        pl.semaphore_signal(barrier, inc=1, device_id=column_peer(d), device_id_type=MESH)
    pl.semaphore_signal(barrier, inc=1, device_id=(before, line), device_id_type=MESH)
    pl.semaphore_signal(barrier, inc=1, device_id=(after, line), device_id_type=MESH)

    started = []

    def send(src, dst, out_sem, in_sem, to):
        copy = pltpu.make_async_remote_copy(
            src_ref=src, dst_ref=dst, send_sem=out_sem, recv_sem=in_sem,
            device_id=to, device_id_type=MESH,
        )
        copy.start()
        started.append(copy)
        return copy

    lane = lanes(W)

    place = lax.broadcasted_iota(jnp.int32, (L, L), 0)
    hot = jnp.where(order[...] == place, 1.0, 0.0).astype(BF16)
    to_cells = jnp.concatenate([hot, hot], axis=1)
    to_lines = jnp.concatenate([hot, hot], axis=0)

    def pair(x):
        return jnp.concatenate(two(x), axis=1)

    def grid(x):
        return lax.dot_general(
            pair(x), to_cells, (((1,), (1,)), ((), ())), preferred_element_type=F32
        )

    def stored(x):
        return mm(pair(x), to_lines)

    def unfold_map(ref, which):
        def load(q):
            return ref[0, :, L * q : L * (q + 1)]

        def store(i, piece):
            tops[which, pl.ds(i, K, stride=C), :] = piece

        unfold(load, store, K)

    for which, ref in enumerate((fwd, piv, bwd)):
        unfold_map(ref, which)

    def prepare(k, carry):
        at = pl.ds(k * C, C)
        fd[k, 0:W, :] = lhs_of(whole_map(tops[0, at, :]))
        fd[k + 1, W : 2 * W, :] = lhs_of(whole_map(tops[1, at, :]))
        bn[k] = lhs_of(-whole_map(tops[2, at, :]))
        for f in range(2):
            st[k, :, L * f : L * (f + 1)] = grid(res[k, pl.ds(f, W, stride=2), :])
        return carry

    lax.fori_loop(0, K, prepare, 0)

    cells_mass = grid(mass[...])
    for f in range(2):
        ph[:, L * f : L * (f + 1)] = freq[f] * cells_mass

    pl.semaphore_wait(barrier, 8)

    def unfold_flux(k, carry):
        def load(q):
            return flux[0, k, :, L * q : L * (q + 1)]

        def store(i, piece):
            xtops[pl.ds(i, 4, stride=C), :] = piece

        unfold(load, store, 4)
        for d in range(4):
            fx[k, d] = lhs_of(whole_map(xtops[d * C : (d + 1) * C, :]))
        return carry

    def pack_back(k, carry):
        tile = ym[k]
        at = pl.ds(pl.multiple_of(k * W, W), W)
        qh[at, 0:256] = lhs_of(real_form(tile, 80))
        qh[at, 256:512] = lhs_of(real_form(tile, 40))
        return carry

    def local_chain(first):
        width = 384 if first else 256
        x = st[0]
        if first:
            top = whole_map(tops[0, 0:C, :])
            x = jnp.concatenate([x, band(roll(top, 80), 80, 120)], axis=1)

        def down(k, x):
            r = mm(fd[k], rhs_of(x))
            zz[k - 1, :, 0:width] = r[W:]
            new = r[:W, 0:256] + st[k]
            if first:
                new = jnp.concatenate([new, r[:W, 256:]], axis=1)
            return new

        x = lax.fori_loop(1, K, down, x)
        heads[0] = x[:, 0:L]
        heads[1] = x[:, L : 2 * L]
        end = mm(fd[K, W : 2 * W, :], rhs_of(x))
        if first:
            back = -whole_map(tops[2, (K - 1) * C : K * C, :])
            end_map = end[:, 256:] + band(roll(back, 40), 40, 80)
            ym[K - 1] = end_map
            end = jnp.concatenate([end[:, :256], end_map], axis=1)
        yl[K - 1] = end[:, :256]

        def climb(step, y):
            k = K - 2 - step
            y = mm(bn[k], rhs_of(y)) + zz[k, :, 0:width]
            yl[k] = y[:, :256]
            if first:
                ym[k] = y[:, 256:]
            return y

        y = lax.fori_loop(0, K - 1, climb, end)
        if first:
            return roll(x[:, 256:], 48) + y[:, 256:]
        return None

    def pack_maps(ref, j, tile):
        ref[j, 0:W, :] = lhs_of(real_form(tile, 0))
        ref[j, W : 2 * W, :] = lhs_of(real_form(tile, 80))
        ref[j, 2 * W : 3 * W, :] = lhs_of(real_form(tile, 40))

    def row_solve(s, first):
        v = [rx[s, j] for j in range(SIDE)]
        join = (lambda a, b: jnp.concatenate([a, b], axis=1)) if first else (lambda a, b: a)
        w = [None, v[0]]
        q = [None]
        if first:
            m = [rxm[j] for j in range(SIDE)]
            wm = [eye_at(80), band(roll(m[0], 80), 80, 120)]
            qm = [band(m[0], 80, 120)]
        for j in range(1, SIDE):
            r = mm(rp[j, 0 : 2 * W, :], rhs_of(join(w[j], wm[j] if first else None)))
            w.append(r[:W, :L] + v[j])
            q.append(r[W:, :L])
            if first:
                wm.append(r[:W, L:])
                qm.append(r[W:, L:])
        y = [None] * SIDE
        cur = v[3] + roll(q[3], 64)
        if first:
            y_map = [None] * SIDE
            y_map[3] = eye_at(40)
            cur_map = band(m[3], 40, 80) + qm[3]
        for j in (2, 1, 0):
            y[j] = cur
            if first:
                y_map[j] = cur_map
            r = mm(rp[j, 2 * W :, :], rhs_of(join(cur, cur_map if first else None)))
            cur = r[:, :L] + v[j]
            if j:
                cur = cur + roll(q[j], 64)
            if first:
                cur_map = r[:, L:] + qm[j]
        half = lane < 64
        for j in range(SIDE):
            lo = w[j] if j else 0.0
            hi = y[j] if j < 3 else 0.0
            ww[j] = jnp.where(half, lo, hi)
        sy[s] = jnp.where(half, w[4], cur)
        if first:
            sym[...] = roll(wm[4], 48) + cur_map
            for j in range(SIDE):
                cw[j] = wm[j] + jnp.where(lane < 80, y_map[j], 0.0)
                cw[j + 4] = band(y_map[j], 80, 120)

    def pack_row(j, carry):
        tile = cw[j]
        dp[j, 0:W, :] = lhs_of(real_form(tile, 80))
        dp[j, W : 2 * W, :] = lhs_of(real_form(tile, 40))
        dp[j, 2 * W :, :] = lhs_of(real_form(cw[j + 4], 80))
        return carry

    def column_solve(s):
        v = [ry[s, j] for j in range(SIDE)]
        w = [None, v[0]]
        q = [None]
        for j in (1, 2):
            r = mm(cp[j, 0 : 2 * W, :], rhs_of(w[j]))
            w.append(r[:W] + v[j])
            q.append(r[W:])
        q.append(mm(cp[3, W : 2 * W, :], rhs_of(w[3])))
        y = [None] * SIDE
        cur = v[3] + roll(q[3], 64)
        for j in (2, 1):
            y[j] = cur
            cur = mm(cp[j, 2 * W :, :], rhs_of(cur)) + v[j] + roll(q[j], 64)
        y[0] = cur
        half = lane < 64
        for j in range(SIDE):
            cw[8 + j] = jnp.where(half, w[j] if j else 0.0, y[j] if j < 3 else 0.0)
        return cw[8 + my_y]

    def edges(m):
        low = high = None
        for i in range(4):
            tile = yl[2 * m + i // 2, :, L * (i % 2) : L * (i % 2 + 1)]
            a, b = roll(tile, 32 * i), roll(tile, 32 * (i + 1))
            low = a if i == 0 else jnp.where(lane >= 32 * i, a, low)
            high = b if i == 0 else jnp.where(lane >= 32 * i, b, high)
        return low, high

    column = lax.rem(lane, SX)

    for s in range(2):
        first = s == 0
        maps = local_chain(first)
        half = lane < 64
        for f in range(2):
            t, u = heads[f], yl[0, :, L * f : L * (f + 1)]
            sx[s, 2 * f] = jnp.where(half, t, roll(u, 64))
            sx[s, 2 * f + 1] = jnp.where(half, roll(t, 64), u)
        copies = []
        if first:
            sxm[...] = maps
        for d in (2, 1, 3):
            copies.append(
                send(sx.at[s, in_row(d)], rx.at[s, my_x], send_x.at[s, d], recv_x.at[s, d], row_peer(d))
            )
            if first:
                copies.append(send(sxm, rxm.at[my_x], send_xm.at[d], recv_xm.at[d], row_peer(d)))
        rx[s, my_x] = sx[s, my_x]
        if first:
            rxm[my_x] = maps
            lax.fori_loop(0, K, pack_back, 0)
        for copy in copies:
            copy.wait_recv()
        if first:
            for j in range(SIDE):
                pack_maps(rp, j, rxm[j])
        row_solve(s, first)

        copies = []
        for d in (2, 1, 3):
            copies.append(send(sy.at[s], ry.at[s, my_y], send_y.at[s, d], recv_y.at[s, d], column_peer(d)))
            if first:
                copies.append(send(sym, rym.at[my_y], send_ym.at[d], recv_ym.at[d], column_peer(d)))
        ry[s, my_y] = sy[s]
        if first:
            rym[my_y] = sym[...]
            lax.fori_loop(0, SIDE, pack_row, 0)
            lax.fori_loop(0, K, unfold_flux, 0)
        for copy in copies:
            copy.wait_recv()
        if first:
            for j in range(SIDE):
                pack_maps(cp, j, rym[j])
        entry = rhs_of(column_solve(s))

        for j in range(SIDE):
            r = mm(dp[j], entry)
            sz[s, j] = ww[j] + jnp.where(half, r[:W], r[W : 2 * W] + roll(r[2 * W :], 64))
        copies = []
        for d in (2, 1, 3):
            copies.append(
                send(sz.at[s, in_row(d)], rz.at[s, my_x], send_z.at[s, d], recv_z.at[s, d], row_peer(d))
            )
        rz[s, my_x] = sz[s, my_x]
        for copy in copies:
            copy.wait_recv()
        z = [rz[s, j] for j in range(SIDE)]
        incoming = jnp.concatenate(
            [jnp.where(half, z[2 * f], roll(z[2 * f + 1], 64)) for f in range(2)], axis=1
        )
        arriving = jnp.concatenate(
            [jnp.where(half, roll(z[2 * f], 64), z[2 * f + 1]) for f in range(2)], axis=1
        )
        both = jnp.concatenate([rhs_of(incoming), rhs_of(arriving)], axis=0)

        low_copies, high_copies = [], []
        for m in range(4):
            r = mm(qh[2 * W * m : 2 * W * (m + 1), :], both)
            for i in range(2):
                k = 2 * m + i
                y = yl[k] + r[W * i : W * (i + 1)]
                yl[k] = y
                upd[k] = RELAXATION * y if first else upd[k] + RELAXATION * y
            low, high = edges(m)
            sl[s, m] = low
            sh[s, m] = high
            high_copies.append(send(sl.at[s, m], hh.at[s, m], send_l.at[s, m], recv_l.at[s, m], (before, line)))
            low_copies.append(send(sh.at[s, m], hl.at[s, m], send_h.at[s, m], recv_h.at[s, m], (after, line)))

        def inner(k, carry):
            y = yl[k]
            ups, downs = [], []
            for f in range(2):
                tile = y[:, L * f : L * (f + 1)]
                ups.append(jnp.where(column > 0, roll(tile, 1), 0.0))
                downs.append(jnp.where(column < SX - 1, roll(tile, -1), 0.0))
            acc = mm(fx[k, 0], rhs_of(jnp.concatenate(ups, axis=1)))
            acc = acc + mm(fx[k, 1], rhs_of(jnp.concatenate(downs, axis=1)))
            turned = jnp.concatenate([-y[C:], y[:C]], axis=0)
            acc = acc + ph[pl.ds(k, 1), :] * turned
            st[k] = KEEP * st[k] - RELAXATION * acc
            if not first:
                for f in range(2):
                    upd_out[k, pl.ds(f, W, stride=2), :] = stored(upd[k, :, L * f : L * (f + 1)])
            return carry

        lax.fori_loop(0, K, inner, 0)

        for m in range(4):
            low_copies[m].wait_recv()
            high_copies[m].wait_recv()
            for i in range(2):
                k = 2 * m + i
                lows, highs = [], []
                for f in range(2):
                    tile = yl[k, :, L * f : L * (f + 1)]
                    slot = 32 * (2 * i + f)
                    lows.append(jnp.where(lane < SX, roll(hl[s, m], -slot), roll(tile, SX)))
                    highs.append(jnp.where(lane >= L - SX, roll(hh[s, m], 96 - slot), roll(tile, -SX)))
                acc = mm(fx[k, 2], rhs_of(jnp.concatenate(lows, axis=1)))
                acc = acc + mm(fx[k, 3], rhs_of(jnp.concatenate(highs, axis=1)))
                current = st[k] - RELAXATION * acc
                if first:
                    st[k] = current
                else:
                    for f in range(2):
                        res_out[k, pl.ds(f, W, stride=2), :] = stored(current[:, L * f : L * (f + 1)])

    for copy in started:
        copy.wait_send()


def shards(residual, forward_maps, pivot_inverse, backward_maps, face_flux, mass_scale, frequencies, line_order):
    vmem = pl.BlockSpec(memory_space=pltpu.VMEM)
    smem = pl.BlockSpec(memory_space=pltpu.SMEM)
    dma = pltpu.SemaphoreType.DMA
    out = jax.ShapeDtypeStruct((K, 2 * W, L), F32)
    update, left = pl.pallas_call(
        kernel,
        out_shape=(out, out),
        in_specs=[vmem, vmem, vmem, vmem, vmem, vmem, smem, vmem],
        out_specs=(vmem, vmem),
        scratch_shapes=[
            pltpu.VMEM((3, K * C, L), F32),
            pltpu.VMEM((4 * C, L), F32),
            pltpu.VMEM((K + 1, 2 * W, 256), BF16),
            pltpu.VMEM((K, W, 256), BF16),
            pltpu.VMEM((K, 4, W, 256), BF16),
            pltpu.VMEM((K * W, 512), BF16),
            pltpu.VMEM((SIDE, 3 * W, 256), BF16),
            pltpu.VMEM((SIDE, 3 * W, 256), BF16),
            pltpu.VMEM((SIDE, 3 * W, 256), BF16),
            pltpu.VMEM((K, W, 256), F32),
            pltpu.VMEM((K, W, 384), F32),
            pltpu.VMEM((K, W, 256), F32),
            pltpu.VMEM((K, W, L), F32),
            pltpu.VMEM((K, W, 256), F32),
            pltpu.VMEM((K, 256), F32),
            pltpu.VMEM((2, W, L), F32),
            pltpu.VMEM((2, SIDE, W, L), F32),
            pltpu.VMEM((2, SIDE, W, L), F32),
            pltpu.VMEM((W, L), F32),
            pltpu.VMEM((SIDE, W, L), F32),
            pltpu.VMEM((2, W, L), F32),
            pltpu.VMEM((2, SIDE, W, L), F32),
            pltpu.VMEM((W, L), F32),
            pltpu.VMEM((SIDE, W, L), F32),
            pltpu.VMEM((2, SIDE, W, L), F32),
            pltpu.VMEM((2, SIDE, W, L), F32),
            pltpu.VMEM((SIDE, W, L), F32),
            pltpu.VMEM((3 * SIDE, W, L), F32),
            pltpu.VMEM((2, 4, W, L), F32),
            pltpu.VMEM((2, 4, W, L), F32),
            pltpu.VMEM((2, 4, W, L), F32),
            pltpu.VMEM((2, 4, W, L), F32),
            dma((2, SIDE)), dma((2, SIDE)), dma((SIDE,)), dma((SIDE,)),
            dma((2, SIDE)), dma((2, SIDE)), dma((SIDE,)), dma((SIDE,)),
            dma((2, SIDE)), dma((2, SIDE)),
            dma((2, 4)), dma((2, 4)), dma((2, 4)), dma((2, 4)),
        ],
        compiler_params=pltpu.CompilerParams(collective_id=0, has_side_effects=True),
        name="sweeps",
    )(
        residual.reshape(K, 2 * W, L), forward_maps, pivot_inverse, backward_maps, face_flux,
        mass_scale, frequencies, line_order.reshape(1, L),
    )
    return update.reshape(K, W, 2, L), left.reshape(K, W, 2, L)


def solution(mesh):
    maps = P("patch", "line", None)
    state = P("line", None, None, "patch")
    placed = (state, maps, maps, maps, P("patch", "line", None, None), P("line", "patch"), P(), P("patch"))
    return jax.shard_map(
        shards, mesh=mesh, in_specs=placed, out_specs=(state, state), check_vma=False
    )
```

```python
import functools

import jax
import jax.numpy as jnp
from jax import lax
from jax.experimental import pallas as pl
from jax.experimental.pallas import tpu as pltpu
from jax.sharding import PartitionSpec as P

SX = 32
RELAXATION = 0.8
KEEP = 1.0 - RELAXATION
C = 40
W = 80
K = 8
L = 128
SIDE = 4
F32 = jnp.float32
BF16 = jnp.bfloat16
MESH = pl.DeviceIdType.MESH


def lanes(rows, width=L):
    return lax.broadcasted_iota(jnp.int32, (rows, width), 1)


def roll(x, by):
    by = by % L
    return x if by == 0 else pltpu.roll(x, by, 1)


def two(x):
    high = x.astype(BF16)
    return high, (x - high.astype(F32)).astype(BF16)


def rhs_of(x):
    high, low = two(x)
    return jnp.concatenate([high, low, high, jnp.zeros((16, x.shape[1]), BF16)], axis=0)


def lhs_of(w):
    lane = lanes(w.shape[0])
    high = w.astype(BF16).astype(F32)
    low = w - high
    moved = roll(high, W)
    first = jnp.where(lane < W, high, moved)
    second = jnp.where(lane < 32, moved, roll(low, 32))
    return jnp.concatenate([first, second], axis=1).astype(BF16)


def real_form(tile, at):
    lane = lanes(W)
    plain = roll(tile, -at)
    moved = roll(tile, C - at)
    turned = jnp.concatenate([-moved[C:], moved[:C]], axis=0)
    return jnp.where(lane < C, plain, jnp.where(lane < W, turned, 0.0))


def whole_map(top):
    lane = lanes(C)
    top = jnp.where(lane < W, top, 0.0)
    bottom = jnp.where(lane < C, -roll(top, -C), jnp.where(lane < W, roll(top, C), 0.0))
    return jnp.concatenate([top, bottom], axis=0)


def mm(a, b):
    return jnp.dot(a, b, preferred_element_type=F32)


def band(x, lo, hi):
    lane = lanes(x.shape[0])
    return jnp.where((lane >= lo) & (lane < hi), x, 0.0)


def eye_at(at):
    row = lax.broadcasted_iota(jnp.int32, (W, L), 0)
    return jnp.where(lanes(W) == row + at, jnp.where(row < C, 1.0, 0.0), 0.0)


def unfold(load, store, rows):
    lane = lanes(rows)
    for group in range(5):
        parts = [load(5 * group + q) for q in range(5)]
        for r in range(8):
            q, off = divmod(W * r, L)
            piece = roll(parts[q], -off)
            if off + W > L:
                piece = jnp.where(lane < L - off, piece, roll(parts[q + 1], -off))
            store(8 * group + r, piece)


def kernel(
    res_in, fwd_in, piv_in, bwd_in, flux_in, mass_in, freq_in, order_in,
    upd_out, res_out,
    res, fwd, piv, bwd, flux, mass, freq, order, load_sem,
    tops, xtops, fd, bn, fx, qh, rp, dp, cp,
    st, zz, yl, ym, upd, ph,
    sx, rx, sxm, rxm, sy, ry, sym, rym, sz, rz, ww, cw,
    sl, sh, hl, hh,
    send_x, recv_x, send_xm, recv_xm, send_y, recv_y, send_ym, recv_ym,
    send_z, recv_z, send_l, recv_l, send_h, recv_h,
):
    patch = lax.axis_index("patch")
    line = lax.axis_index("line")
    patches = lax.axis_size("patch")
    my_y, my_x = line // SIDE, line % SIDE
    before = lax.rem(patch + patches - 1, patches)
    after = lax.rem(patch + 1, patches)

    def in_row(d):
        return lax.rem(my_x + d, SIDE)

    def in_column(d):
        return lax.rem(my_y + d, SIDE)

    def row_peer(d):
        return (patch, my_y * SIDE + in_row(d))

    def column_peer(d):
        return (patch, in_column(d) * SIDE + my_x)

    barrier = pltpu.get_barrier_semaphore()
    for d in range(1, SIDE):
        pl.semaphore_signal(barrier, inc=1, device_id=row_peer(d), device_id_type=MESH)
        pl.semaphore_signal(barrier, inc=1, device_id=column_peer(d), device_id_type=MESH)
    pl.semaphore_signal(barrier, inc=1, device_id=(before, line), device_id_type=MESH)
    pl.semaphore_signal(barrier, inc=1, device_id=(after, line), device_id_type=MESH)

    half_map = C * W
    loads = [
        pltpu.make_async_copy(a, b, load_sem.at[i])
        for i, (a, b) in enumerate((
            (fwd_in.at[0, :, 0:half_map], fwd),
            (order_in, order),
            (res_in, res),
            (piv_in.at[0, :, 0:half_map], piv),
            (bwd_in.at[0, :, 0:half_map], bwd),
            (mass_in, mass),
            (freq_in, freq),
            (flux_in.at[0, :, :, 0:half_map], flux),
        ))
    ]
    for copy in loads:
        copy.start()

    started = []

    def send(src, dst, out_sem, in_sem, to):
        copy = pltpu.make_async_remote_copy(
            src_ref=src, dst_ref=dst, send_sem=out_sem, recv_sem=in_sem,
            device_id=to, device_id_type=MESH,
        )
        copy.start()
        started.append(copy)
        return copy

    lane = lanes(W)

    def unfold_map(ref, which):
        def load(q):
            return ref[:, L * q : L * (q + 1)]

        def store(i, piece):
            tops[which, pl.ds(i, K, stride=C), :] = piece

        unfold(load, store, K)

    loads[0].wait()
    unfold_map(fwd, 0)
    loads[1].wait()

    place = lax.broadcasted_iota(jnp.int32, (L, L), 0)
    hot = jnp.where(order[...] == place, 1.0, 0.0).astype(BF16)
    to_cells = jnp.concatenate([hot, hot], axis=1)
    to_lines = jnp.concatenate([hot, hot], axis=0)

    def pair(x):
        return jnp.concatenate(two(x), axis=1)

    def grid(x):
        return lax.dot_general(
            pair(x), to_cells, (((1,), (1,)), ((), ())), preferred_element_type=F32
        )

    def stored(x):
        return mm(pair(x), to_lines)

    def top_of(which, k):
        return whole_map(tops[which, k * C : (k + 1) * C, :])

    def pack_down(k):
        if k < K:
            fd[k, 0:W, :] = lhs_of(top_of(0, k))
            for f in range(2):
                st[k, :, L * f : L * (f + 1)] = grid(res[k, pl.ds(f, W, stride=2), :])
        fd[k, W : 2 * W, :] = lhs_of(top_of(1, k - 1))
        bn[k - 1] = lhs_of(-top_of(2, k - 1))

    loads[2].wait()
    loads[3].wait()
    unfold_map(piv, 1)
    loads[4].wait()
    unfold_map(bwd, 2)
    for f in range(2):
        st[0, :, L * f : L * (f + 1)] = grid(res[0, pl.ds(f, W, stride=2), :])
    pack_down(1)

    def unfold_flux(k, carry):
        def load(q):
            return flux[k, :, L * q : L * (q + 1)]

        def store(i, piece):
            xtops[pl.ds(i, 4, stride=C), :] = piece

        unfold(load, store, 4)
        for d in range(4):
            fx[k, d * W : (d + 1) * W, :] = lhs_of(whole_map(xtops[d * C : (d + 1) * C, :]))
        return carry

    def pack_back(k, carry):
        tile = ym[k]
        at = pl.ds(pl.multiple_of(k * W, W), W)
        qh[at, 0:256] = lhs_of(real_form(tile, 80))
        qh[at, 256:512] = lhs_of(real_form(tile, 40))
        return carry

    def step_down(k, x):
        r = mm(fd[k], rhs_of(x))
        zz[k - 1, :, 0 : x.shape[1]] = r[W:]
        new = r[:W, 0:256] + st[k]
        if x.shape[1] > 256:
            new = jnp.concatenate([new, r[:W, 256:]], axis=1)
        return new

    def local_back(x):
        first = x.shape[1] > 256
        end = mm(fd[K, W : 2 * W, :], rhs_of(x))
        if first:
            end_map = end[:, 256:] + band(roll(-top_of(2, K - 1), 40), 40, 80)
            ym[K - 1] = end_map
            end = jnp.concatenate([end[:, :256], end_map], axis=1)
        yl[K - 1] = end[:, :256]
        y = end
        for k in range(K - 2, -1, -1):
            y = mm(bn[k], rhs_of(y)) + zz[k, :, 0 : x.shape[1]]
            yl[k] = y[:, :256]
            if first:
                ym[k] = y[:, 256:]
        if first:
            return y, roll(x[:, 256:], 48) + y[:, 256:]
        return y, None

    def pack_maps(ref, j, tile):
        ref[j, 0:W, :] = lhs_of(real_form(tile, 0))
        ref[j, W : 2 * W, :] = lhs_of(real_form(tile, 80))
        ref[j, 2 * W : 3 * W, :] = lhs_of(real_form(tile, 40))

    def row_solve(s, first):
        v = [rx[s, j] for j in range(SIDE)]
        join = (lambda a, b: jnp.concatenate([a, b], axis=1)) if first else (lambda a, b: a)
        w = [None, v[0]]
        q = [None]
        if first:
            m = [rxm[j] for j in range(SIDE)]
            wm = [eye_at(80), band(roll(m[0], 80), 80, 120)]
            qm = [band(m[0], 80, 120)]
        for j in range(1, SIDE):
            r = mm(rp[j, 0 : 2 * W, :], rhs_of(join(w[j], wm[j] if first else None)))
            w.append(r[:W, :L] + v[j])
            q.append(r[W:, :L])
            if first:
                wm.append(r[:W, L:])
                qm.append(r[W:, L:])
        y = [None] * SIDE
        cur = v[3] + roll(q[3], 64)
        if first:
            y_map = [None] * SIDE
            y_map[3] = eye_at(40)
            cur_map = band(m[3], 40, 80) + qm[3]
        for j in (2, 1, 0):
            y[j] = cur
            if first:
                y_map[j] = cur_map
            r = mm(rp[j, 2 * W :, :], rhs_of(join(cur, cur_map if first else None)))
            cur = r[:, :L] + v[j]
            if j:
                cur = cur + roll(q[j], 64)
            if first:
                cur_map = r[:, L:] + qm[j]
        half = lane < 64
        for j in range(SIDE):
            lo = w[j] if j else 0.0
            hi = y[j] if j < 3 else 0.0
            ww[j] = jnp.where(half, lo, hi)
        sy[s] = jnp.where(half, w[4], cur)
        if first:
            sym[...] = roll(wm[4], 48) + cur_map
            for j in range(SIDE):
                cw[j] = wm[j] + jnp.where(lane < 80, y_map[j], 0.0)
                cw[j + 4] = band(y_map[j], 80, 120)

    def pack_row(j, carry):
        tile = cw[j]
        dp[j, 0:W, :] = lhs_of(real_form(tile, 80))
        dp[j, W : 2 * W, :] = lhs_of(real_form(tile, 40))
        dp[j, 2 * W :, :] = lhs_of(real_form(cw[j + 4], 80))
        return carry

    def column_solve(s):
        v = [ry[s, j] for j in range(SIDE)]
        w = [None, v[0]]
        q = [None]
        for j in (1, 2):
            r = mm(cp[j, 0 : 2 * W, :], rhs_of(w[j]))
            w.append(r[:W] + v[j])
            q.append(r[W:])
        q.append(mm(cp[3, W : 2 * W, :], rhs_of(w[3])))
        y = [None] * SIDE
        cur = v[3] + roll(q[3], 64)
        for j in (2, 1):
            y[j] = cur
            cur = mm(cp[j, 2 * W :, :], rhs_of(cur)) + v[j] + roll(q[j], 64)
        y[0] = cur
        half = lane < 64
        for j in range(SIDE):
            cw[8 + j] = jnp.where(half, w[j] if j else 0.0, y[j] if j < 3 else 0.0)
        return cw[8 + my_y]

    def edges(m):
        low = high = None
        for i in range(4):
            tile = yl[2 * m + i // 2, :, L * (i % 2) : L * (i % 2 + 1)]
            a, b = roll(tile, 32 * i), roll(tile, 32 * (i + 1))
            low = a if i == 0 else jnp.where(lane >= 32 * i, a, low)
            high = b if i == 0 else jnp.where(lane >= 32 * i, b, high)
        return low, high

    column = lax.rem(lane, SX)

    for s in range(2):
        first = s == 0
        if first:
            x = jnp.concatenate([st[0], band(roll(top_of(0, 0), 80), 80, 120)], axis=1)
            for k in range(1, K):
                pack_down(k + 1)
                x = step_down(k, x)
            pl.semaphore_wait(barrier, 8)
        y, maps = local_back(x)
        half = lane < 64
        for f in range(2):
            t, u = x[:, L * f : L * (f + 1)], y[:, L * f : L * (f + 1)]
            sx[s, 2 * f] = jnp.where(half, t, roll(u, 64))
            sx[s, 2 * f + 1] = jnp.where(half, roll(t, 64), u)
        copies = []
        if first:
            sxm[...] = maps
        for d in (2, 1, 3):
            copies.append(
                send(sx.at[s, in_row(d)], rx.at[s, my_x], send_x.at[s, d], recv_x.at[s, d], row_peer(d))
            )
            if first:
                copies.append(send(sxm, rxm.at[my_x], send_xm.at[d], recv_xm.at[d], row_peer(d)))
        rx[s, my_x] = sx[s, my_x]
        if first:
            rxm[my_x] = maps
            lax.fori_loop(0, K, pack_back, 0)
            loads[5].wait()
            loads[6].wait()
            cells_mass = grid(mass[...])
            for f in range(2):
                ph[:, L * f : L * (f + 1)] = freq[f] * cells_mass
        for copy in copies:
            copy.wait_recv()
        if first:
            for j in range(SIDE):
                pack_maps(rp, j, rxm[j])
        row_solve(s, first)

        copies = []
        for d in (2, 1, 3):
            copies.append(send(sy.at[s], ry.at[s, my_y], send_y.at[s, d], recv_y.at[s, d], column_peer(d)))
            if first:
                copies.append(send(sym, rym.at[my_y], send_ym.at[d], recv_ym.at[d], column_peer(d)))
        ry[s, my_y] = sy[s]
        if first:
            rym[my_y] = sym[...]
            lax.fori_loop(0, SIDE, pack_row, 0)
            loads[7].wait()
            lax.fori_loop(0, K, unfold_flux, 0)
        for copy in copies:
            copy.wait_recv()
        if first:
            for j in range(SIDE):
                pack_maps(cp, j, rym[j])
        entry = rhs_of(column_solve(s))

        for j in range(SIDE):
            r = mm(dp[j], entry)
            sz[s, j] = ww[j] + jnp.where(half, r[:W], r[W : 2 * W] + roll(r[2 * W :], 64))
        copies = []
        for d in (2, 1, 3):
            copies.append(
                send(sz.at[s, in_row(d)], rz.at[s, my_x], send_z.at[s, d], recv_z.at[s, d], row_peer(d))
            )
        rz[s, my_x] = sz[s, my_x]
        for copy in copies:
            copy.wait_recv()
        z = [rz[s, j] for j in range(SIDE)]
        incoming = jnp.concatenate(
            [jnp.where(half, z[2 * f], roll(z[2 * f + 1], 64)) for f in range(2)], axis=1
        )
        arriving = jnp.concatenate(
            [jnp.where(half, roll(z[2 * f], 64), z[2 * f + 1]) for f in range(2)], axis=1
        )
        both = jnp.concatenate([rhs_of(incoming), rhs_of(arriving)], axis=0)

        low_copies, high_copies = [], []
        for m in range(4):
            r = mm(qh[2 * W * m : 2 * W * (m + 1), :], both)
            for i in range(2):
                k = 2 * m + i
                y = yl[k] + r[W * i : W * (i + 1)]
                yl[k] = y
                upd[k] = RELAXATION * y if first else upd[k] + RELAXATION * y
            low, high = edges(m)
            sl[s, m] = low
            sh[s, m] = high
            high_copies.append(send(sl.at[s, m], hh.at[s, m], send_l.at[s, m], recv_l.at[s, m], (before, line)))
            low_copies.append(send(sh.at[s, m], hl.at[s, m], send_h.at[s, m], recv_h.at[s, m], (after, line)))

        def inner(k, carry):
            y = yl[k]
            r = mm(fx[k], rhs_of(y))
            parts = []
            for f in range(2):
                at = slice(L * f, L * (f + 1))
                acc = jnp.where(column > 0, roll(r[0:W, at], 1), 0.0)
                acc = acc + jnp.where(column < SX - 1, roll(r[W : 2 * W, at], -1), 0.0)
                acc = acc + jnp.where(lane >= SX, roll(r[2 * W : 3 * W, at], SX), 0.0)
                acc = acc + jnp.where(lane < L - SX, roll(r[3 * W :, at], -SX), 0.0)
                parts.append(acc)
            turned = jnp.concatenate([-y[C:], y[:C]], axis=0)
            acc = jnp.concatenate(parts, axis=1) + ph[pl.ds(k, 1), :] * turned
            st[k] = KEEP * st[k] - RELAXATION * acc
            if not first:
                for f in range(2):
                    upd_out[k, pl.ds(f, W, stride=2), :] = stored(upd[k, :, L * f : L * (f + 1)])
            return carry

        lax.fori_loop(0, K, inner, 0)

        for m in range(4):
            low_copies[m].wait_recv()
            high_copies[m].wait_recv()
            k0, k1 = 2 * m, 2 * m + 1
            r_low = mm(jnp.concatenate([fx[k0, 2 * W : 3 * W, :], fx[k1, 2 * W : 3 * W, :]], axis=0), rhs_of(hl[s, m]))
            r_high = mm(jnp.concatenate([fx[k0, 3 * W :, :], fx[k1, 3 * W :, :]], axis=0), rhs_of(hh[s, m]))
            for i in range(2):
                k = 2 * m + i
                parts = []
                for f in range(2):
                    slot = 32 * (2 * i + f)
                    low = roll(r_low[W * i : W * (i + 1)], -slot)
                    high = roll(r_high[W * i : W * (i + 1)], 96 - slot)
                    parts.append(jnp.where(lane < SX, low, jnp.where(lane >= L - SX, high, 0.0)))
                current = st[k] - RELAXATION * jnp.concatenate(parts, axis=1)
                if first:
                    st[k] = current
                    x = step_down(k, x) if k else current
                else:
                    for f in range(2):
                        res_out[k, pl.ds(f, W, stride=2), :] = stored(current[:, L * f : L * (f + 1)])

    for copy in started:
        copy.wait_send()


def shards(residual, forward_maps, pivot_inverse, backward_maps, face_flux, mass_scale, frequencies, line_order):
    vmem = pl.BlockSpec(memory_space=pltpu.VMEM)
    anywhere = pl.BlockSpec(memory_space=pl.ANY)
    dma = pltpu.SemaphoreType.DMA
    out = pltpu.VMEM((K, 2 * W, L), F32)
    update, left = pl.pallas_call(
        kernel,
        out_shape=(out, out),
        in_specs=[anywhere] * 8,
        out_specs=(vmem, vmem),
        scratch_shapes=[
            pltpu.VMEM((K, 2 * W, L), F32),
            pltpu.VMEM((K, C * W), F32),
            pltpu.VMEM((K, C * W), F32),
            pltpu.VMEM((K, C * W), F32),
            pltpu.VMEM((K, 4, C * W), F32),
            pltpu.VMEM((K, L), F32),
            pltpu.SMEM((2,), F32),
            pltpu.VMEM((1, L), jnp.int32),
            dma((8,)),
            pltpu.VMEM((3, K * C, L), F32),
            pltpu.VMEM((4 * C, L), F32),
            pltpu.VMEM((K + 1, 2 * W, 256), BF16),
            pltpu.VMEM((K, W, 256), BF16),
            pltpu.VMEM((K, 4 * W, 256), BF16),
            pltpu.VMEM((K * W, 512), BF16),
            pltpu.VMEM((SIDE, 3 * W, 256), BF16),
            pltpu.VMEM((SIDE, 3 * W, 256), BF16),
            pltpu.VMEM((SIDE, 3 * W, 256), BF16),
            pltpu.VMEM((K, W, 256), F32),
            pltpu.VMEM((K, W, 384), F32),
            pltpu.VMEM((K, W, 256), F32),
            pltpu.VMEM((K, W, L), F32),
            pltpu.VMEM((K, W, 256), F32),
            pltpu.VMEM((K, 256), F32),
            pltpu.VMEM((2, SIDE, W, L), F32),
            pltpu.VMEM((2, SIDE, W, L), F32),
            pltpu.VMEM((W, L), F32),
            pltpu.VMEM((SIDE, W, L), F32),
            pltpu.VMEM((2, W, L), F32),
            pltpu.VMEM((2, SIDE, W, L), F32),
            pltpu.VMEM((W, L), F32),
            pltpu.VMEM((SIDE, W, L), F32),
            pltpu.VMEM((2, SIDE, W, L), F32),
            pltpu.VMEM((2, SIDE, W, L), F32),
            pltpu.VMEM((SIDE, W, L), F32),
            pltpu.VMEM((3 * SIDE, W, L), F32),
            pltpu.VMEM((2, 4, W, L), F32),
            pltpu.VMEM((2, 4, W, L), F32),
            pltpu.VMEM((2, 4, W, L), F32),
            pltpu.VMEM((2, 4, W, L), F32),
            dma((2, SIDE)), dma((2, SIDE)), dma((SIDE,)), dma((SIDE,)),
            dma((2, SIDE)), dma((2, SIDE)), dma((SIDE,)), dma((SIDE,)),
            dma((2, SIDE)), dma((2, SIDE)),
            dma((2, 4)), dma((2, 4)), dma((2, 4)), dma((2, 4)),
        ],
        compiler_params=pltpu.CompilerParams(collective_id=0, has_side_effects=True),
        name="sweeps",
    )(
        residual.reshape(K, 2 * W, L), forward_maps, pivot_inverse, backward_maps, face_flux,
        mass_scale, frequencies, line_order.reshape(1, L),
    )
    return update.reshape(K, W, 2, L), left.reshape(K, W, 2, L)


def solution(mesh):
    maps = P("patch", "line", None)
    state = P("line", None, None, "patch")
    placed = (state, maps, maps, maps, P("patch", "line", None, None), P("line", "patch"), P(), P("patch"))
    return jax.shard_map(
        shards, mesh=mesh, in_specs=placed, out_specs=(state, state), check_vma=False
    )
```

```python
import functools

import jax
import jax.numpy as jnp
from jax import lax
from jax.experimental import pallas as pl
from jax.experimental.pallas import tpu as pltpu
from jax.sharding import PartitionSpec as P

SX = 32
RELAXATION = 0.8
KEEP = 1.0 - RELAXATION
C = 40
W = 80
K = 8
L = 128
SIDE = 4
F32 = jnp.float32
BF16 = jnp.bfloat16
MESH = pl.DeviceIdType.MESH


def lanes(rows, width=L):
    return lax.broadcasted_iota(jnp.int32, (rows, width), 1)


def roll(x, by):
    by = by % L
    return x if by == 0 else pltpu.roll(x, by, 1)


def two(x):
    high = x.astype(BF16)
    return high, (x - high.astype(F32)).astype(BF16)


def rhs_of(x):
    high, low = two(x)
    return jnp.concatenate([high, low, high, jnp.zeros((16, x.shape[1]), BF16)], axis=0)


def lhs_of(w):
    lane = lanes(w.shape[0])
    high = w.astype(BF16).astype(F32)
    low = w - high
    moved = roll(high, W)
    first = jnp.where(lane < W, high, moved)
    second = jnp.where(lane < 32, moved, roll(low, 32))
    return jnp.concatenate([first, second], axis=1).astype(BF16)


def real_form(tile, at):
    lane = lanes(W)
    plain = roll(tile, -at)
    moved = roll(tile, C - at)
    turned = jnp.concatenate([-moved[C:], moved[:C]], axis=0)
    return jnp.where(lane < C, plain, jnp.where(lane < W, turned, 0.0))


def whole_map(top):
    lane = lanes(C)
    top = jnp.where(lane < W, top, 0.0)
    bottom = jnp.where(lane < C, -roll(top, -C), jnp.where(lane < W, roll(top, C), 0.0))
    return jnp.concatenate([top, bottom], axis=0)


def mm(a, b):
    return jnp.dot(a, b, preferred_element_type=F32)


def band(x, lo, hi):
    lane = lanes(x.shape[0])
    return jnp.where((lane >= lo) & (lane < hi), x, 0.0)


def eye_at(at):
    row = lax.broadcasted_iota(jnp.int32, (W, L), 0)
    return jnp.where(lanes(W) == row + at, jnp.where(row < C, 1.0, 0.0), 0.0)


def unfold(load, store, rows):
    lane = lanes(rows)
    for group in range(5):
        parts = [load(5 * group + q) for q in range(5)]
        for r in range(8):
            q, off = divmod(W * r, L)
            piece = roll(parts[q], -off)
            if off + W > L:
                piece = jnp.where(lane < L - off, piece, roll(parts[q + 1], -off))
            store(8 * group + r, piece)


def kernel(
    res_in, fwd_in, piv_in, bwd_in, flux_in, mass_in, freq_in, order_in,
    upd_out, res_out,
    res, fwd, piv, bwd, flux, mass, freq, order, load_sem,
    tops, xtops, fd, bn, fx, qh, rp, dp, cp,
    st, zz, yl, ym, upd, ph,
    stx, rtx, sux, rux, sty, rty, suy, ruy, swz, rwz, syz, ryz, yloc, cw, pick,
    sl, sh, hl, hh,
    out_tx, in_tx, out_ux, in_ux, out_ty, in_ty, out_uy, in_uy,
    out_wz, in_wz, out_yz, in_yz, send_l, recv_l, send_h, recv_h,
):
    patch = lax.axis_index("patch")
    line = lax.axis_index("line")
    patches = lax.axis_size("patch")
    my_y, my_x = line // SIDE, line % SIDE
    before = lax.rem(patch + patches - 1, patches)
    after = lax.rem(patch + 1, patches)

    def in_row(d):
        return lax.rem(my_x + d, SIDE)

    def in_column(d):
        return lax.rem(my_y + d, SIDE)

    def row_peer(d):
        return (patch, my_y * SIDE + in_row(d))

    def column_peer(d):
        return (patch, in_column(d) * SIDE + my_x)

    barrier = pltpu.get_barrier_semaphore()
    for d in range(1, SIDE):
        pl.semaphore_signal(barrier, inc=1, device_id=row_peer(d), device_id_type=MESH)
        pl.semaphore_signal(barrier, inc=1, device_id=column_peer(d), device_id_type=MESH)
    pl.semaphore_signal(barrier, inc=1, device_id=(before, line), device_id_type=MESH)
    pl.semaphore_signal(barrier, inc=1, device_id=(after, line), device_id_type=MESH)

    half_map = C * W
    loads = [
        pltpu.make_async_copy(a, b, load_sem.at[i])
        for i, (a, b) in enumerate((
            (fwd_in.at[0, :, 0:half_map], fwd),
            (order_in, order),
            (res_in, res),
            (piv_in.at[0, :, 0:half_map], piv),
            (bwd_in.at[0, :, 0:half_map], bwd),
            (mass_in, mass),
            (freq_in, freq),
            (flux_in.at[0, :, :, 0:half_map], flux),
        ))
    ]
    for copy in loads:
        copy.start()

    started = []

    def send(src, dst, out_sem, in_sem, to):
        copy = pltpu.make_async_remote_copy(
            src_ref=src, dst_ref=dst, send_sem=out_sem, recv_sem=in_sem,
            device_id=to, device_id_type=MESH,
        )
        copy.start()
        started.append(copy)
        return copy

    lane = lanes(W)

    def unfold_map(ref, which):
        def load(q):
            return ref[:, L * q : L * (q + 1)]

        def store(i, piece):
            tops[which, pl.ds(i, K, stride=C), :] = piece

        unfold(load, store, K)

    loads[0].wait()
    unfold_map(fwd, 0)
    loads[1].wait()

    place = lax.broadcasted_iota(jnp.int32, (L, L), 0)
    hot = jnp.where(order[...] == place, 1.0, 0.0).astype(BF16)
    to_cells = jnp.concatenate([hot, hot], axis=1)
    to_lines = jnp.concatenate([hot, hot], axis=0)

    def pair(x):
        return jnp.concatenate(two(x), axis=1)

    def grid(x):
        return lax.dot_general(
            pair(x), to_cells, (((1,), (1,)), ((), ())), preferred_element_type=F32
        )

    def stored(x):
        return mm(pair(x), to_lines)

    def top_of(which, k):
        return whole_map(tops[which, k * C : (k + 1) * C, :])

    def pack_down(k):
        if k < K:
            fd[k, 0:W, :] = lhs_of(top_of(0, k))
            for f in range(2):
                st[k, :, L * f : L * (f + 1)] = grid(res[k, pl.ds(f, W, stride=2), :])
        fd[k, W : 2 * W, :] = lhs_of(top_of(1, k - 1))
        bn[k - 1] = lhs_of(-top_of(2, k - 1))

    loads[2].wait()
    loads[3].wait()
    unfold_map(piv, 1)
    loads[4].wait()
    unfold_map(bwd, 2)
    for f in range(2):
        st[0, :, L * f : L * (f + 1)] = grid(res[0, pl.ds(f, W, stride=2), :])
    pack_down(1)

    def unfold_flux(k, carry):
        def load(q):
            return flux[k, :, L * q : L * (q + 1)]

        def store(i, piece):
            xtops[pl.ds(i, 4, stride=C), :] = piece

        unfold(load, store, 4)
        for d in range(4):
            fx[k, d * W : (d + 1) * W, :] = lhs_of(whole_map(xtops[d * C : (d + 1) * C, :]))
        return carry

    def pack_back(k, carry):
        tile = ym[k]
        at = pl.ds(pl.multiple_of(k * W, W), W)
        qh[0, at, :] = lhs_of(real_form(tile, 80))
        qh[1, at, :] = lhs_of(real_form(tile, 40))
        return carry

    def step_down(k, x):
        r = mm(fd[k], rhs_of(x))
        zz[k - 1, :, 0 : x.shape[1]] = r[W:]
        new = r[:W, 0:256] + st[k]
        if x.shape[1] > 256:
            new = jnp.concatenate([new, r[:W, 256:]], axis=1)
        return new

    def local_back(x):
        first = x.shape[1] > 256
        end = mm(fd[K, W : 2 * W, :], rhs_of(x))
        if first:
            end_map = end[:, 256:] + band(roll(-top_of(2, K - 1), 40), 40, 80)
            ym[K - 1] = end_map
            end = jnp.concatenate([end[:, :256], end_map], axis=1)
        yl[K - 1] = end[:, :256]
        y = end
        for k in range(K - 2, -1, -1):
            y = mm(bn[k], rhs_of(y)) + zz[k, :, 0 : x.shape[1]]
            yl[k] = y[:, :256]
            if first:
                ym[k] = y[:, 256:]
        if first:
            return y, roll(x[:, 256:], 48) + y[:, 256:]
        return y, None

    def fold_low(x):
        return jnp.where(lanes(C) < 64, x[:C], roll(x[C:], 64))

    def fold_high(x):
        return jnp.where(lanes(C) < 64, roll(x[:C], 64), x[C:])

    def unfold_low(x):
        return jnp.concatenate([x, roll(x, 64)], axis=0)

    def join(x, extra):
        return x if extra is None else jnp.concatenate([x, extra], axis=1)

    def pack_row(j, carry):
        at = pl.ds(pl.multiple_of(j * W, W), W)
        tile = cw[j]
        dp[0, at, :] = lhs_of(real_form(tile, 80))
        dp[1, at, :] = lhs_of(real_form(cw[j + SIDE], 80))
        dp[2, at, :] = lhs_of(real_form(tile, 40))
        return carry

    def to_row(src, dst, out_sem, in_sem):
        copies = [send(src(in_row(d)), dst(my_x), out_sem.at[d], in_sem.at[d], row_peer(d)) for d in (2, 1, 3)]
        dst(my_x)[...] = src(my_x)[...]
        return copies

    def to_column(src, dst, out_sem, in_sem):
        copies = [send(src, dst(my_y), out_sem.at[d], in_sem.at[d], column_peer(d)) for d in (2, 1, 3)]
        dst(my_y)[...] = src[...]
        return copies

    def arrived(copies):
        for copy in copies:
            copy.wait_recv()

    def edges(m):
        low = high = None
        for i in range(4):
            tile = yl[2 * m + i // 2, :, L * (i % 2) : L * (i % 2 + 1)]
            a, b = roll(tile, 32 * i), roll(tile, 32 * (i + 1))
            low = a if i == 0 else jnp.where(lane >= 32 * i, a, low)
            high = b if i == 0 else jnp.where(lane >= 32 * i, b, high)
        return low, high

    column = lax.rem(lane, SX)

    for s in range(2):
        first = s == 0
        if first:
            x = jnp.concatenate([st[0], band(roll(top_of(0, 0), 80), 80, 120)], axis=1)
            for k in range(1, K):
                pack_down(k + 1)
                x = step_down(k, x)
            pl.semaphore_wait(barrier, 8)
        for f in range(2):
            t = x[:, L * f : L * (f + 1)]
            stx[s, 2 * f, 0:C, :] = fold_low(t)
            stx[s, 2 * f + 1, 0:C, :] = fold_high(t)
        if first:
            fold = fold_low(roll(x[:, 256:], 48))
            for j in range(SIDE):
                stx[s, j, C:W, :] = fold
        rows = W if first else C
        t_copies = to_row(
            lambda j: stx.at[s, j, 0:rows], lambda j: rtx.at[s, j, 0:rows], out_tx.at[s], in_tx.at[s]
        )

        y, maps = local_back(x)
        for f in range(2):
            u = y[:, L * f : L * (f + 1)]
            sux[s, 2 * f, 0:C, :] = fold_low(u)
            sux[s, 2 * f + 1, 0:C, :] = fold_high(u)
        if first:
            for j in range(SIDE):
                sux[s, j, C:, :] = maps
        back_rows = W + C if first else C
        u_copies = to_row(
            lambda j: sux.at[s, j, 0:back_rows], lambda j: rux.at[s, j, 0:back_rows], out_ux.at[s], in_ux.at[s]
        )
        if first:
            lax.fori_loop(0, K, pack_back, 0)
            loads[5].wait()
            loads[6].wait()
            cells_mass = grid(mass[...])
            for f in range(2):
                ph[:, L * f : L * (f + 1)] = freq[f] * cells_mass

        arrived(t_copies)
        t = [unfold_low(rtx[s, j, 0:C, :]) for j in range(SIDE)]
        w, wm, w_rhs, q, qm = [None, t[0]], [None] * 5, [None], [None], [None] * SIDE
        if first:
            m = [unfold_low(rtx[s, j, C:W, :]) for j in range(SIDE)]
            for j in range(1, SIDE):
                rp[j, 0:W, :] = lhs_of(real_form(m[j], 0))
            wm[0:2] = [eye_at(80), band(roll(m[0], 80), 80, 120)]
        for j in range(1, SIDE):
            w_rhs.append(rhs_of(join(w[j], wm[j])))
            r = mm(rp[j, 0 : W if first else 2 * W, :], w_rhs[j])
            w.append(r[:W, :L] + t[j])
            if first:
                wm[j + 1] = r[:, L:]
            else:
                q.append(r[W:])
        sty[s, 0:C, :] = fold_low(w[4])
        if first:
            sty[s, C:W, :] = fold_low(roll(wm[4], 48))
        t_copies = to_column(
            sty.at[s, 0:rows], lambda j: rty.at[s, j, 0:rows], out_ty.at[s], in_ty.at[s]
        )

        arrived(u_copies)
        u = [unfold_low(rux[s, j, 0:C, :]) for j in range(SIDE)]
        v, vm = [None] * SIDE, [None] * SIDE
        cur_map = None
        if first:
            nq = [rux[s, j, C:, :] for j in range(SIDE)]
            qm[0] = band(nq[0], 80, 120)
            for j in range(1, SIDE):
                rp[j, W : 2 * W, :] = lhs_of(real_form(nq[j], 80))
                r = mm(rp[j, W : 2 * W, :], w_rhs[j])
                q.append(r[:, :L])
                qm[j] = r[:, L:]
            for j in range(SIDE - 1):
                rp[j, 2 * W :, :] = lhs_of(real_form(nq[j], 40))
            vm[3] = eye_at(40)
            cur_map = band(nq[3], 40, 80) + qm[3]
        cur = u[3] + q[3]
        for j in (2, 1, 0):
            v[j], vm[j] = cur, cur_map
            r = mm(rp[j, 2 * W :, :], rhs_of(join(cur, cur_map)))
            cur = r[:, :L] + u[j]
            if j:
                cur = cur + q[j]
            if first:
                cur_map = r[:, L:] + qm[j]
        suy[s, 0:C, :] = fold_low(cur)
        if first:
            suy[s, C:, :] = cur_map
        u_copies = to_column(
            suy.at[s, 0:back_rows], lambda j: ruy.at[s, j, 0:back_rows], out_uy.at[s], in_uy.at[s]
        )
        if first:
            for j in range(SIDE):
                cw[j] = wm[j] + band(vm[j], 40, 80)
                cw[j + SIDE] = vm[j]
            lax.fori_loop(0, SIDE, pack_row, 0)
            loads[7].wait()
            lax.fori_loop(0, K // 2, unfold_flux, 0)
        w_own, v_own = w, v

        arrived(t_copies)
        t = [unfold_low(rty[s, j, 0:C, :]) for j in range(SIDE)]
        if first:
            for j in (1, 2):
                cp[j, 0:W, :] = lhs_of(real_form(unfold_low(rty[s, j, C:W, :]), 0))
        w, w_rhs, q = [jnp.zeros((W, L), F32), t[0]], [None], [None]
        for j in (1, 2):
            w_rhs.append(rhs_of(w[j]))
            r = mm(cp[j, 0 : W if first else 2 * W, :], w_rhs[j])
            w.append(r[:W] + t[j])
            if not first:
                q.append(r[W:])
        w_rhs.append(rhs_of(w[3]))
        for j in range(SIDE):
            pick[j] = w[j]
        entry = rhs_of(pick[my_y])
        r = mm(dp[0], entry)
        for j in range(SIDE):
            into = r[W * j : W * (j + 1)]
            swz[s, j] = fold_low(into + w_own[j] if j else into)
        t_copies = to_row(lambda j: swz.at[s, j], lambda j: rwz.at[s, j], out_wz.at[s], in_wz.at[s])
        r = mm(dp[1], entry)
        for j in range(SIDE):
            into = r[W * j : W * (j + 1)]
            yloc[j] = into + v_own[j] if j < 3 else into
        if not first:
            q.append(mm(cp[3, W : 2 * W, :], w_rhs[3]))

        arrived(u_copies)
        u = [unfold_low(ruy[s, j, 0:C, :]) for j in range(SIDE)]
        if first:
            nq = [ruy[s, j, C:, :] for j in range(SIDE)]
            for j in range(1, SIDE):
                cp[j, W : 2 * W, :] = lhs_of(real_form(nq[j], 80))
                q.append(mm(cp[j, W : 2 * W, :], w_rhs[j]))
            for j in (1, 2):
                cp[j, 2 * W :, :] = lhs_of(real_form(nq[j], 40))
        pick[3] = jnp.zeros((W, L), F32)
        cur = u[3] + q[3]
        for j in (2, 1):
            pick[j] = cur
            cur = mm(cp[j, 2 * W :, :], rhs_of(cur)) + u[j] + q[j]
        pick[0] = cur
        r = mm(dp[2], rhs_of(pick[my_y]))
        for j in range(SIDE):
            syz[s, j] = fold_low(r[W * j : W * (j + 1)] + yloc[j])
        u_copies = to_row(lambda j: syz.at[s, j], lambda j: ryz.at[s, j], out_yz.at[s], in_yz.at[s])
        if first:
            lax.fori_loop(K // 2, K, unfold_flux, 0)

        def assemble(ref):
            tiles = []
            for f in range(2):
                a, b = ref[s, 2 * f], ref[s, 2 * f + 1]
                tiles.append(
                    jnp.concatenate(
                        [jnp.where(lanes(C) < 64, a, roll(b, 64)), jnp.where(lanes(C) < 64, roll(a, 64), b)], axis=0
                    )
                )
            return jnp.concatenate(tiles, axis=1)

        arrived(t_copies)
        incoming = rhs_of(assemble(rwz))
        for m in range(4):
            r = mm(qh[0, 2 * W * m : 2 * W * (m + 1), :], incoming)
            for i in range(2):
                yl[2 * m + i] = yl[2 * m + i] + r[W * i : W * (i + 1)]
        arrived(u_copies)
        arriving = rhs_of(assemble(ryz))

        low_copies, high_copies = [], []
        for m in range(4):
            r = mm(qh[1, 2 * W * m : 2 * W * (m + 1), :], arriving)
            for i in range(2):
                k = 2 * m + i
                y = yl[k] + r[W * i : W * (i + 1)]
                yl[k] = y
                upd[k] = RELAXATION * y if first else upd[k] + RELAXATION * y
            low, high = edges(m)
            sl[s, m] = low
            sh[s, m] = high
            high_copies.append(send(sl.at[s, m], hh.at[s, m], send_l.at[s, m], recv_l.at[s, m], (before, line)))
            low_copies.append(send(sh.at[s, m], hl.at[s, m], send_h.at[s, m], recv_h.at[s, m], (after, line)))

        def inner(k, carry):
            y = yl[k]
            r = mm(fx[k], rhs_of(y))
            parts = []
            for f in range(2):
                at = slice(L * f, L * (f + 1))
                acc = jnp.where(column > 0, roll(r[0:W, at], 1), 0.0)
                acc = acc + jnp.where(column < SX - 1, roll(r[W : 2 * W, at], -1), 0.0)
                acc = acc + jnp.where(lane >= SX, roll(r[2 * W : 3 * W, at], SX), 0.0)
                acc = acc + jnp.where(lane < L - SX, roll(r[3 * W :, at], -SX), 0.0)
                parts.append(acc)
            turned = jnp.concatenate([-y[C:], y[:C]], axis=0)
            acc = jnp.concatenate(parts, axis=1) + ph[pl.ds(k, 1), :] * turned
            st[k] = KEEP * st[k] - RELAXATION * acc
            if not first:
                for f in range(2):
                    upd_out[k, pl.ds(f, W, stride=2), :] = stored(upd[k, :, L * f : L * (f + 1)])
            return carry

        lax.fori_loop(0, K, inner, 0)

        for m in range(4):
            low_copies[m].wait_recv()
            high_copies[m].wait_recv()
            k0, k1 = 2 * m, 2 * m + 1
            r_low = mm(jnp.concatenate([fx[k0, 2 * W : 3 * W, :], fx[k1, 2 * W : 3 * W, :]], axis=0), rhs_of(hl[s, m]))
            r_high = mm(jnp.concatenate([fx[k0, 3 * W :, :], fx[k1, 3 * W :, :]], axis=0), rhs_of(hh[s, m]))
            for i in range(2):
                k = 2 * m + i
                parts = []
                for f in range(2):
                    slot = 32 * (2 * i + f)
                    low = roll(r_low[W * i : W * (i + 1)], -slot)
                    high = roll(r_high[W * i : W * (i + 1)], 96 - slot)
                    parts.append(jnp.where(lane < SX, low, jnp.where(lane >= L - SX, high, 0.0)))
                current = st[k] - RELAXATION * jnp.concatenate(parts, axis=1)
                if first:
                    st[k] = current
                    x = step_down(k, x) if k else current
                else:
                    for f in range(2):
                        res_out[k, pl.ds(f, W, stride=2), :] = stored(current[:, L * f : L * (f + 1)])

    for copy in started:
        copy.wait_send()


def shards(residual, forward_maps, pivot_inverse, backward_maps, face_flux, mass_scale, frequencies, line_order):
    vmem = pl.BlockSpec(memory_space=pltpu.VMEM)
    anywhere = pl.BlockSpec(memory_space=pl.ANY)
    dma = pltpu.SemaphoreType.DMA
    out = pltpu.VMEM((K, 2 * W, L), F32)
    update, left = pl.pallas_call(
        kernel,
        out_shape=(out, out),
        in_specs=[anywhere] * 8,
        out_specs=(vmem, vmem),
        scratch_shapes=[
            pltpu.VMEM((K, 2 * W, L), F32),
            pltpu.VMEM((K, C * W), F32),
            pltpu.VMEM((K, C * W), F32),
            pltpu.VMEM((K, C * W), F32),
            pltpu.VMEM((K, 4, C * W), F32),
            pltpu.VMEM((K, L), F32),
            pltpu.SMEM((2,), F32),
            pltpu.VMEM((1, L), jnp.int32),
            dma((8,)),
            pltpu.VMEM((3, K * C, L), F32),
            pltpu.VMEM((4 * C, L), F32),
            pltpu.VMEM((K + 1, 2 * W, 256), BF16),
            pltpu.VMEM((K, W, 256), BF16),
            pltpu.VMEM((K, 4 * W, 256), BF16),
            pltpu.VMEM((2, K * W, 256), BF16),
            pltpu.VMEM((SIDE, 3 * W, 256), BF16),
            pltpu.VMEM((3, SIDE * W, 256), BF16),
            pltpu.VMEM((SIDE, 3 * W, 256), BF16),
            pltpu.VMEM((K, W, 256), F32),
            pltpu.VMEM((K, W, 384), F32),
            pltpu.VMEM((K, W, 256), F32),
            pltpu.VMEM((K, W, L), F32),
            pltpu.VMEM((K, W, 256), F32),
            pltpu.VMEM((K, 256), F32),
            pltpu.VMEM((2, SIDE, W, L), F32), pltpu.VMEM((2, SIDE, W, L), F32),
            pltpu.VMEM((2, SIDE, W + C, L), F32), pltpu.VMEM((2, SIDE, W + C, L), F32),
            pltpu.VMEM((2, W, L), F32), pltpu.VMEM((2, SIDE, W, L), F32),
            pltpu.VMEM((2, W + C, L), F32), pltpu.VMEM((2, SIDE, W + C, L), F32),
            pltpu.VMEM((2, SIDE, C, L), F32), pltpu.VMEM((2, SIDE, C, L), F32),
            pltpu.VMEM((2, SIDE, C, L), F32), pltpu.VMEM((2, SIDE, C, L), F32),
            pltpu.VMEM((SIDE, W, L), F32),
            pltpu.VMEM((2 * SIDE, W, L), F32), pltpu.VMEM((SIDE, W, L), F32),
            pltpu.VMEM((2, 4, W, L), F32),
            pltpu.VMEM((2, 4, W, L), F32),
            pltpu.VMEM((2, 4, W, L), F32),
            pltpu.VMEM((2, 4, W, L), F32),
            *[dma((2, SIDE)) for _ in range(12)],
            dma((2, 4)), dma((2, 4)), dma((2, 4)), dma((2, 4)),
        ],
        compiler_params=pltpu.CompilerParams(collective_id=0, has_side_effects=True),
        name="sweeps",
    )(
        residual.reshape(K, 2 * W, L), forward_maps, pivot_inverse, backward_maps, face_flux,
        mass_scale, frequencies, line_order.reshape(1, L),
    )
    return update.reshape(K, W, 2, L), left.reshape(K, W, 2, L)


def solution(mesh):
    maps = P("patch", "line", None)
    state = P("line", None, None, "patch")
    placed = (state, maps, maps, maps, P("patch", "line", None, None), P("line", "patch"), P(), P("patch"))
    return jax.shard_map(
        shards, mesh=mesh, in_specs=placed, out_specs=(state, state), check_vma=False
    )
```

```python
import functools

import jax
import jax.numpy as jnp
from jax import lax
from jax.experimental import pallas as pl
from jax.experimental.pallas import tpu as pltpu
from jax.sharding import PartitionSpec as P

SX = 32
RELAXATION = 0.8
KEEP = 1.0 - RELAXATION
C = 40
W = 80
K = 8
L = 128
SIDE = 4
F32 = jnp.float32
BF16 = jnp.bfloat16
MESH = pl.DeviceIdType.MESH


def lanes(rows, width=L):
    return lax.broadcasted_iota(jnp.int32, (rows, width), 1)


def roll(x, by):
    by = by % L
    return x if by == 0 else pltpu.roll(x, by, 1)


def two(x):
    high = x.astype(BF16)
    return high, (x - high.astype(F32)).astype(BF16)


def rhs_of(x):
    high, low = two(x)
    return jnp.concatenate([high, low, high, jnp.zeros((16, x.shape[1]), BF16)], axis=0)


def lhs_of(w):
    lane = lanes(w.shape[0])
    high = w.astype(BF16).astype(F32)
    low = w - high
    moved = roll(high, W)
    first = jnp.where(lane < W, high, moved)
    second = jnp.where(lane < 32, moved, roll(low, 32))
    return jnp.concatenate([first, second], axis=1).astype(BF16)


def real_form(tile, at):
    lane = lanes(W)
    plain = roll(tile, -at)
    moved = roll(tile, C - at)
    turned = jnp.concatenate([-moved[C:], moved[:C]], axis=0)
    return jnp.where(lane < C, plain, jnp.where(lane < W, turned, 0.0))


def whole_map(top):
    lane = lanes(C)
    top = jnp.where(lane < W, top, 0.0)
    bottom = jnp.where(lane < C, -roll(top, -C), jnp.where(lane < W, roll(top, C), 0.0))
    return jnp.concatenate([top, bottom], axis=0)


def mm(a, b):
    return jnp.dot(a, b, preferred_element_type=F32)


def band(x, lo, hi):
    lane = lanes(x.shape[0])
    return jnp.where((lane >= lo) & (lane < hi), x, 0.0)


def eye_at(at):
    row = lax.broadcasted_iota(jnp.int32, (W, L), 0)
    return jnp.where(lanes(W) == row + at, jnp.where(row < C, 1.0, 0.0), 0.0)


def unfold(load, store, rows):
    lane = lanes(rows)
    for group in range(5):
        parts = [load(5 * group + q) for q in range(5)]
        for r in range(8):
            q, off = divmod(W * r, L)
            piece = roll(parts[q], -off)
            if off + W > L:
                piece = jnp.where(lane < L - off, piece, roll(parts[q + 1], -off))
            store(8 * group + r, piece)


def kernel(
    res_in, fwd_in, piv_in, bwd_in, flux_in, mass_in, freq_in, order_in,
    upd_out, res_out,
    res, fwd, piv, bwd, flux, mass, freq, order, load_sem,
    tops, xtops, fd, bn, fx, qh, rp, dp, cp,
    st, zz, yl, ym, upd, ph,
    stx, rtx, sux, rux, sty, rty, suy, ruy, swz, rwz, syz, ryz, yloc, cw, pick,
    sl, sh, hl, hh,
    out_tx, in_tx, out_ux, in_ux, out_ty, in_ty, out_uy, in_uy,
    out_wz, in_wz, out_yz, in_yz, send_l, recv_l, send_h, recv_h,
):
    patch = lax.axis_index("patch")
    line = lax.axis_index("line")
    patches = lax.axis_size("patch")
    my_y, my_x = line // SIDE, line % SIDE
    before = lax.rem(patch + patches - 1, patches)
    after = lax.rem(patch + 1, patches)

    def in_row(d):
        return lax.rem(my_x + d, SIDE)

    def in_column(d):
        return lax.rem(my_y + d, SIDE)

    def row_peer(d):
        return (patch, my_y * SIDE + in_row(d))

    def column_peer(d):
        return (patch, in_column(d) * SIDE + my_x)

    barrier = pltpu.get_barrier_semaphore()
    for d in range(1, SIDE):
        pl.semaphore_signal(barrier, inc=1, device_id=row_peer(d), device_id_type=MESH)
        pl.semaphore_signal(barrier, inc=1, device_id=column_peer(d), device_id_type=MESH)
    pl.semaphore_signal(barrier, inc=1, device_id=(before, line), device_id_type=MESH)
    pl.semaphore_signal(barrier, inc=1, device_id=(after, line), device_id_type=MESH)

    half_map = C * W
    loads = [
        pltpu.make_async_copy(a, b, load_sem.at[i])
        for i, (a, b) in enumerate((
            (fwd_in.at[0, :, 0:half_map], fwd),
            (order_in, order),
            (res_in, res),
            (piv_in.at[0, :, 0:half_map], piv),
            (bwd_in.at[0, :, 0:half_map], bwd),
            (mass_in, mass),
            (freq_in, freq),
            (flux_in.at[0, :, :, 0:half_map], flux),
        ))
    ]
    for copy in loads:
        copy.start()

    sent = []

    def send(src, dst, out_sem, in_sem, to):
        copy = pltpu.make_async_remote_copy(
            src_ref=src, dst_ref=dst, send_sem=out_sem, recv_sem=in_sem,
            device_id=to, device_id_type=MESH,
        )
        copy.start()
        return copy

    lane = lanes(W)

    def unfold_map(ref, which):
        def load(q):
            return ref[:, L * q : L * (q + 1)]

        def store(i, piece):
            tops[which, pl.ds(i, K, stride=C), :] = piece

        unfold(load, store, K)

    loads[0].wait()
    unfold_map(fwd, 0)
    loads[1].wait()

    place = lax.broadcasted_iota(jnp.int32, (L, L), 0)
    hot = jnp.where(order[...] == place, 1.0, 0.0).astype(BF16)
    to_cells = jnp.concatenate([hot, hot], axis=1)
    to_lines = jnp.concatenate([hot, hot], axis=0)

    def pair(x):
        return jnp.concatenate(two(x), axis=1)

    def grid(x):
        return lax.dot_general(
            pair(x), to_cells, (((1,), (1,)), ((), ())), preferred_element_type=F32
        )

    def stored(x):
        return mm(pair(x), to_lines)

    def top_of(which, k):
        return whole_map(tops[which, k * C : (k + 1) * C, :])

    def to_grid(k):
        r = grid(jnp.concatenate([res[k, pl.ds(f, W, stride=2), :] for f in range(2)], axis=0))
        st[k] = jnp.concatenate([r[:W], r[W:]], axis=1)

    def pack_down(k):
        if k < K:
            fd[k, 0:W, :] = lhs_of(top_of(0, k))
            to_grid(k)
        fd[k, W : 2 * W, :] = lhs_of(top_of(1, k - 1))
        bn[k - 1] = lhs_of(-top_of(2, k - 1))

    loads[2].wait()
    loads[3].wait()
    unfold_map(piv, 1)
    loads[4].wait()
    unfold_map(bwd, 2)
    to_grid(0)
    pack_down(1)

    def unfold_flux(k, carry):
        def load(q):
            return flux[k, :, L * q : L * (q + 1)]

        def store(i, piece):
            xtops[pl.ds(i, 4, stride=C), :] = piece

        unfold(load, store, 4)
        for d in range(4):
            fx[k, d * W : (d + 1) * W, :] = lhs_of(whole_map(xtops[d * C : (d + 1) * C, :]))
        return carry

    def pack_back(k, carry):
        tile = ym[k]
        at = pl.ds(pl.multiple_of(k * W, W), W)
        qh[0, at, :] = lhs_of(real_form(tile, 80))
        qh[1, at, :] = lhs_of(real_form(tile, 40))
        return carry

    def step_down(k, x):
        r = mm(fd[k], rhs_of(x))
        zz[k - 1, :, 0 : x.shape[1]] = r[W:]
        new = r[:W, 0:256] + st[k]
        if x.shape[1] > 256:
            new = jnp.concatenate([new, r[:W, 256:]], axis=1)
        return new

    def local_back(x):
        first = x.shape[1] > 256
        end = mm(fd[K, W : 2 * W, :], rhs_of(x))
        if first:
            end_map = end[:, 256:] + band(roll(-top_of(2, K - 1), 40), 40, 80)
            ym[K - 1] = end_map
            end = jnp.concatenate([end[:, :256], end_map], axis=1)
        yl[K - 1] = end[:, :256]
        y = end
        for k in range(K - 2, -1, -1):
            y = mm(bn[k], rhs_of(y)) + zz[k, :, 0 : x.shape[1]]
            yl[k] = y[:, :256]
            if first:
                ym[k] = y[:, 256:]
        if first:
            return y, roll(x[:, 256:], 48) + y[:, 256:]
        return y, None

    def fold_low(x):
        return jnp.where(lanes(C) < 64, x[:C], roll(x[C:], 64))

    def fold_high(x):
        return jnp.where(lanes(C) < 64, roll(x[:C], 64), x[C:])

    def unfold_low(x):
        return jnp.concatenate([x, roll(x, 64)], axis=0)

    def join(x, extra):
        return x if extra is None else jnp.concatenate([x, extra], axis=1)

    def pack_row(j, carry):
        at = pl.ds(pl.multiple_of(j * W, W), W)
        tile = cw[j]
        dp[0, at, :] = lhs_of(real_form(tile, 80))
        dp[1, at, :] = lhs_of(real_form(cw[j + SIDE], 80))
        dp[2, at, :] = lhs_of(real_form(tile, 40))
        return carry

    def to_row(src, dst, three, out_sem, in_sem):
        for d in (2, 1, 3):
            send(src(in_row(d)), dst(my_x), out_sem, in_sem, row_peer(d))
        dst(my_x)[...] = src(my_x)[...]
        sent.append((three, out_sem))
        return three, in_sem

    def to_column(src, dst, three, out_sem, in_sem):
        for d in (2, 1, 3):
            send(src, dst(my_y), out_sem, in_sem, column_peer(d))
        dst(my_y)[...] = src[...]
        sent.append((three, out_sem))
        return three, in_sem

    def bytes_of(ref, sem):
        pltpu.make_async_copy(ref, ref, sem).wait()

    def arrived(copies):
        bytes_of(*copies)

    def edges(pieces):
        low = high = None
        for i, tile in enumerate(pieces):
            a, b = roll(tile, 32 * i), roll(tile, 32 * (i + 1))
            low = a if i == 0 else jnp.where(lane >= 32 * i, a, low)
            high = b if i == 0 else jnp.where(lane >= 32 * i, b, high)
        return low, high

    column = lax.rem(lane, SX)

    for s in range(2):
        first = s == 0
        if first:
            x = jnp.concatenate([st[0], band(roll(top_of(0, 0), 80), 80, 120)], axis=1)
            for k in range(1, K):
                pack_down(k + 1)
                x = step_down(k, x)
            pl.semaphore_wait(barrier, 8)
        for f in range(2):
            t = x[:, L * f : L * (f + 1)]
            stx[s, 2 * f, 0:C, :] = fold_low(t)
            stx[s, 2 * f + 1, 0:C, :] = fold_high(t)
        if first:
            fold = fold_low(roll(x[:, 256:], 48))
            for j in range(SIDE):
                stx[s, j, C:W, :] = fold
        rows = W if first else C
        t_copies = to_row(
            lambda j: stx.at[s, j, 0:rows], lambda j: rtx.at[s, j, 0:rows],
            rtx.at[s, 0:3, 0:rows], out_tx.at[s], in_tx.at[s]
        )

        y, maps = local_back(x)
        for f in range(2):
            u = y[:, L * f : L * (f + 1)]
            sux[s, 2 * f, 0:C, :] = fold_low(u)
            sux[s, 2 * f + 1, 0:C, :] = fold_high(u)
        if first:
            for j in range(SIDE):
                sux[s, j, C:, :] = maps
        back_rows = W + C if first else C
        u_copies = to_row(
            lambda j: sux.at[s, j, 0:back_rows], lambda j: rux.at[s, j, 0:back_rows],
            rux.at[s, 0:3, 0:back_rows], out_ux.at[s], in_ux.at[s]
        )
        if first:
            lax.fori_loop(0, K, pack_back, 0)
            loads[5].wait()
            loads[6].wait()
            cells_mass = grid(mass[...])
            for f in range(2):
                ph[:, L * f : L * (f + 1)] = freq[f] * cells_mass

        arrived(t_copies)
        t = [unfold_low(rtx[s, j, 0:C, :]) for j in range(SIDE)]
        w, wm, w_rhs, q, qm = [None, t[0]], [None] * 5, [None], [None], [None] * SIDE
        if first:
            m = [unfold_low(rtx[s, j, C:W, :]) for j in range(SIDE)]
            for j in range(1, SIDE):
                rp[j, 0:W, :] = lhs_of(real_form(m[j], 0))
            wm[0:2] = [eye_at(80), band(roll(m[0], 80), 80, 120)]
        for j in range(1, SIDE):
            w_rhs.append(rhs_of(join(w[j], wm[j])))
            r = mm(rp[j, 0 : W if first else 2 * W, :], w_rhs[j])
            w.append(r[:W, :L] + t[j])
            if first:
                wm[j + 1] = r[:, L:]
            else:
                q.append(r[W:])
        sty[s, 0:C, :] = fold_low(w[4])
        if first:
            sty[s, C:W, :] = fold_low(roll(wm[4], 48))
        t_copies = to_column(
            sty.at[s, 0:rows], lambda j: rty.at[s, j, 0:rows],
            rty.at[s, 0:3, 0:rows], out_ty.at[s], in_ty.at[s]
        )

        arrived(u_copies)
        u = [unfold_low(rux[s, j, 0:C, :]) for j in range(SIDE)]
        v, vm = [None] * SIDE, [None] * SIDE
        cur_map = None
        if first:
            nq = [rux[s, j, C:, :] for j in range(SIDE)]
            qm[0] = band(nq[0], 80, 120)
            for j in range(1, SIDE):
                rp[j, W : 2 * W, :] = lhs_of(real_form(nq[j], 80))
                r = mm(rp[j, W : 2 * W, :], w_rhs[j])
                q.append(r[:, :L])
                qm[j] = r[:, L:]
            for j in range(SIDE - 1):
                rp[j, 2 * W :, :] = lhs_of(real_form(nq[j], 40))
            vm[3] = eye_at(40)
            cur_map = band(nq[3], 40, 80) + qm[3]
        cur = u[3] + q[3]
        for j in (2, 1, 0):
            v[j], vm[j] = cur, cur_map
            r = mm(rp[j, 2 * W :, :], rhs_of(join(cur, cur_map)))
            cur = r[:, :L] + u[j]
            if j:
                cur = cur + q[j]
            if first:
                cur_map = r[:, L:] + qm[j]
        suy[s, 0:C, :] = fold_low(cur)
        if first:
            suy[s, C:, :] = cur_map
        u_copies = to_column(
            suy.at[s, 0:back_rows], lambda j: ruy.at[s, j, 0:back_rows],
            ruy.at[s, 0:3, 0:back_rows], out_uy.at[s], in_uy.at[s]
        )
        if first:
            for j in range(SIDE):
                cw[j] = wm[j] + band(vm[j], 40, 80)
                cw[j + SIDE] = vm[j]
            lax.fori_loop(0, SIDE, pack_row, 0)
            loads[7].wait()
            lax.fori_loop(0, K // 2, unfold_flux, 0)
        w_own, v_own = w, v

        arrived(t_copies)
        t = [unfold_low(rty[s, j, 0:C, :]) for j in range(SIDE)]
        if first:
            for j in (1, 2):
                cp[j, 0:W, :] = lhs_of(real_form(unfold_low(rty[s, j, C:W, :]), 0))
        w, w_rhs, q = [jnp.zeros((W, L), F32), t[0]], [None], [None]
        for j in (1, 2):
            w_rhs.append(rhs_of(w[j]))
            r = mm(cp[j, 0 : W if first else 2 * W, :], w_rhs[j])
            w.append(r[:W] + t[j])
            if not first:
                q.append(r[W:])
        w_rhs.append(rhs_of(w[3]))
        for j in range(SIDE):
            pick[j] = w[j]
        entry = rhs_of(pick[my_y])
        r = mm(dp[0], entry)
        for j in range(SIDE):
            into = r[W * j : W * (j + 1)]
            swz[s, j] = fold_low(into + w_own[j] if j else into)
        t_copies = to_row(lambda j: swz.at[s, j], lambda j: rwz.at[s, j], rwz.at[s, 0:3], out_wz.at[s], in_wz.at[s])
        r = mm(dp[1], entry)
        for j in range(SIDE):
            into = r[W * j : W * (j + 1)]
            yloc[j] = into + v_own[j] if j < 3 else into
        if not first:
            q.append(mm(cp[3, W : 2 * W, :], w_rhs[3]))

        arrived(u_copies)
        u = [unfold_low(ruy[s, j, 0:C, :]) for j in range(SIDE)]
        if first:
            nq = [ruy[s, j, C:, :] for j in range(SIDE)]
            for j in range(1, SIDE):
                cp[j, W : 2 * W, :] = lhs_of(real_form(nq[j], 80))
                q.append(mm(cp[j, W : 2 * W, :], w_rhs[j]))
            for j in (1, 2):
                cp[j, 2 * W :, :] = lhs_of(real_form(nq[j], 40))
        pick[3] = jnp.zeros((W, L), F32)
        cur = u[3] + q[3]
        for j in (2, 1):
            pick[j] = cur
            cur = mm(cp[j, 2 * W :, :], rhs_of(cur)) + u[j] + q[j]
        pick[0] = cur
        r = mm(dp[2], rhs_of(pick[my_y]))
        for j in range(SIDE):
            syz[s, j] = fold_low(r[W * j : W * (j + 1)] + yloc[j])
        u_copies = to_row(lambda j: syz.at[s, j], lambda j: ryz.at[s, j], ryz.at[s, 0:3], out_yz.at[s], in_yz.at[s])
        if first:
            lax.fori_loop(K // 2, K, unfold_flux, 0)

        def assemble(ref):
            tiles = []
            for f in range(2):
                a, b = ref[s, 2 * f], ref[s, 2 * f + 1]
                tiles.append(
                    jnp.concatenate(
                        [jnp.where(lanes(C) < 64, a, roll(b, 64)), jnp.where(lanes(C) < 64, roll(a, 64), b)], axis=0
                    )
                )
            return jnp.concatenate(tiles, axis=1)

        arrived(t_copies)
        incoming = rhs_of(assemble(rwz))
        for m in range(4):
            r = mm(qh[0, 2 * W * m : 2 * W * (m + 1), :], incoming)
            for i in range(2):
                yl[2 * m + i] = yl[2 * m + i] + r[W * i : W * (i + 1)]
        arrived(u_copies)
        arriving = rhs_of(assemble(ryz))

        def last(m):
            return mm(qh[1, 2 * W * m : 2 * W * (m + 1), :], arriving)

        low_copies, high_copies = [], []
        following = last(0)
        for m in range(4):
            r, following = following, last(m + 1) if m < 3 else None
            pieces = []
            for i in range(2):
                k = 2 * m + i
                y = yl[k] + r[W * i : W * (i + 1)]
                yl[k] = y
                upd[k] = RELAXATION * y if first else upd[k] + RELAXATION * y
                pieces += [y[:, :L], y[:, L:]]
            low, high = edges(pieces)
            sl[s, m] = low
            sh[s, m] = high
            high_copies.append(send(sl.at[s, m], hh.at[s, m], send_l.at[s], recv_l.at[s, m], (before, line)))
            low_copies.append(send(sh.at[s, m], hl.at[s, m], send_h.at[s], recv_h.at[s, m], (after, line)))
        sent.append((sl.at[s], send_l.at[s]))
        sent.append((sh.at[s], send_h.at[s]))

        def inner(m, carry):
            ys = [yl[2 * m + i] for i in range(2)]
            rs = [mm(fx[2 * m + i], rhs_of(ys[i])) for i in range(2)]
            for i in range(2):
                k, y, r = 2 * m + i, ys[i], rs[i]
                parts = []
                for f in range(2):
                    at = slice(L * f, L * (f + 1))
                    acc = jnp.where(column > 0, roll(r[0:W, at], 1), 0.0)
                    acc = acc + jnp.where(column < SX - 1, roll(r[W : 2 * W, at], -1), 0.0)
                    acc = acc + jnp.where(lane >= SX, roll(r[2 * W : 3 * W, at], SX), 0.0)
                    acc = acc + jnp.where(lane < L - SX, roll(r[3 * W :, at], -SX), 0.0)
                    parts.append(acc)
                turned = jnp.concatenate([-y[C:], y[:C]], axis=0)
                acc = jnp.concatenate(parts, axis=1) + ph[pl.ds(k, 1), :] * turned
                st[k] = KEEP * st[k] - RELAXATION * acc
            return carry

        lax.fori_loop(0, K // 2, inner, 0)

        def put(out, k, x):
            r = stored(jnp.concatenate([x[:, :L], x[:, L:]], axis=0))
            for f in range(2):
                out[k, pl.ds(f, W, stride=2), :] = r[W * f : W * (f + 1)]

        if not first:

            def put_update(k, carry):
                put(upd_out, k, upd[k])
                return carry

            lax.fori_loop(0, K, put_update, 0, unroll=4)

        def across(m):
            low_copies[m].wait_recv()
            high_copies[m].wait_recv()
            k0, k1 = 2 * m, 2 * m + 1
            low = jnp.concatenate([fx[k0, 2 * W : 3 * W, :], fx[k1, 2 * W : 3 * W, :]], axis=0)
            high = jnp.concatenate([fx[k0, 3 * W :, :], fx[k1, 3 * W :, :]], axis=0)
            return mm(low, rhs_of(hl[s, m])), mm(high, rhs_of(hh[s, m]))

        following = across(0)
        for m in range(4):
            (r_low, r_high), following = following, across(m + 1) if m < 3 else None
            for i in range(2):
                k = 2 * m + i
                parts = []
                for f in range(2):
                    slot = 32 * (2 * i + f)
                    low = roll(r_low[W * i : W * (i + 1)], -slot)
                    high = roll(r_high[W * i : W * (i + 1)], 96 - slot)
                    parts.append(jnp.where(lane < SX, low, jnp.where(lane >= L - SX, high, 0.0)))
                current = st[k] - RELAXATION * jnp.concatenate(parts, axis=1)
                if first:
                    st[k] = current
                    x = step_down(k, x) if k else current
                else:
                    put(res_out, k, current)

    for ref, sem in sent:
        bytes_of(ref, sem)


def shards(residual, forward_maps, pivot_inverse, backward_maps, face_flux, mass_scale, frequencies, line_order):
    vmem = pl.BlockSpec(memory_space=pltpu.VMEM)
    anywhere = pl.BlockSpec(memory_space=pl.ANY)
    dma = pltpu.SemaphoreType.DMA
    out = pltpu.VMEM((K, 2 * W, L), F32)
    update, left = pl.pallas_call(
        kernel,
        out_shape=(out, out),
        in_specs=[anywhere] * 8,
        out_specs=(vmem, vmem),
        scratch_shapes=[
            pltpu.VMEM((K, 2 * W, L), F32),
            pltpu.VMEM((K, C * W), F32),
            pltpu.VMEM((K, C * W), F32),
            pltpu.VMEM((K, C * W), F32),
            pltpu.VMEM((K, 4, C * W), F32),
            pltpu.VMEM((K, L), F32),
            pltpu.SMEM((2,), F32),
            pltpu.VMEM((1, L), jnp.int32),
            dma((8,)),
            pltpu.VMEM((3, K * C, L), F32),
            pltpu.VMEM((4 * C, L), F32),
            pltpu.VMEM((K + 1, 2 * W, 256), BF16),
            pltpu.VMEM((K, W, 256), BF16),
            pltpu.VMEM((K, 4 * W, 256), BF16),
            pltpu.VMEM((2, K * W, 256), BF16),
            pltpu.VMEM((SIDE, 3 * W, 256), BF16),
            pltpu.VMEM((3, SIDE * W, 256), BF16),
            pltpu.VMEM((SIDE, 3 * W, 256), BF16),
            pltpu.VMEM((K, W, 256), F32),
            pltpu.VMEM((K, W, 384), F32),
            pltpu.VMEM((K, W, 256), F32),
            pltpu.VMEM((K, W, L), F32),
            pltpu.VMEM((K, W, 256), F32),
            pltpu.VMEM((K, 256), F32),
            pltpu.VMEM((2, SIDE, W, L), F32), pltpu.VMEM((2, SIDE, W, L), F32),
            pltpu.VMEM((2, SIDE, W + C, L), F32), pltpu.VMEM((2, SIDE, W + C, L), F32),
            pltpu.VMEM((2, W, L), F32), pltpu.VMEM((2, SIDE, W, L), F32),
            pltpu.VMEM((2, W + C, L), F32), pltpu.VMEM((2, SIDE, W + C, L), F32),
            pltpu.VMEM((2, SIDE, C, L), F32), pltpu.VMEM((2, SIDE, C, L), F32),
            pltpu.VMEM((2, SIDE, C, L), F32), pltpu.VMEM((2, SIDE, C, L), F32),
            pltpu.VMEM((SIDE, W, L), F32),
            pltpu.VMEM((2 * SIDE, W, L), F32), pltpu.VMEM((SIDE, W, L), F32),
            pltpu.VMEM((2, 4, W, L), F32),
            pltpu.VMEM((2, 4, W, L), F32),
            pltpu.VMEM((2, 4, W, L), F32),
            pltpu.VMEM((2, 4, W, L), F32),
            *[dma((2,)) for _ in range(12)],
            dma((2,)), dma((2, 4)), dma((2,)), dma((2, 4)),
        ],
        compiler_params=pltpu.CompilerParams(collective_id=0, has_side_effects=True),
        name="sweeps",
    )(
        residual.reshape(K, 2 * W, L), forward_maps, pivot_inverse, backward_maps, face_flux,
        mass_scale, frequencies, line_order.reshape(1, L),
    )
    return update.reshape(K, W, 2, L), left.reshape(K, W, 2, L)


def solution(mesh):
    maps = P("patch", "line", None)
    state = P("line", None, None, "patch")
    placed = (state, maps, maps, maps, P("patch", "line", None, None), P("line", "patch"), P(), P("patch"))
    return jax.shard_map(
        shards, mesh=mesh, in_specs=placed, out_specs=(state, state), check_vma=False
    )
```

```python
import functools

import jax
import jax.numpy as jnp
from jax import lax
from jax.experimental import pallas as pl
from jax.experimental.pallas import tpu as pltpu
from jax.sharding import PartitionSpec as P

SX = 32
RELAXATION = 0.8
KEEP = 1.0 - RELAXATION
C = 40
W = 80
K = 8
L = 128
SIDE = 4
F32 = jnp.float32
BF16 = jnp.bfloat16
MESH = pl.DeviceIdType.MESH


def lanes(rows, width=L):
    return lax.broadcasted_iota(jnp.int32, (rows, width), 1)


def roll(x, by):
    by = by % L
    return x if by == 0 else pltpu.roll(x, by, 1)


def two(x):
    high = x.astype(BF16)
    return high, (x - high.astype(F32)).astype(BF16)


def rhs_of(x):
    high, low = two(x)
    return jnp.concatenate([high, low, high, jnp.zeros((16, x.shape[1]), BF16)], axis=0)


def lhs_of(w):
    lane = lanes(w.shape[0])
    high = w.astype(BF16).astype(F32)
    low = w - high
    moved = roll(high, W)
    first = jnp.where(lane < W, high, moved)
    second = jnp.where(lane < 32, moved, roll(low, 32))
    return jnp.concatenate([first, second], axis=1).astype(BF16)


def real_form(tile, at):
    lane = lanes(W)
    plain = roll(tile, -at)
    moved = roll(tile, C - at)
    turned = jnp.concatenate([-moved[C:], moved[:C]], axis=0)
    return jnp.where(lane < C, plain, jnp.where(lane < W, turned, 0.0))


def whole_map(top):
    lane = lanes(C)
    top = jnp.where(lane < W, top, 0.0)
    bottom = jnp.where(lane < C, -roll(top, -C), jnp.where(lane < W, roll(top, C), 0.0))
    return jnp.concatenate([top, bottom], axis=0)


def mm(a, b):
    return jnp.dot(a, b, preferred_element_type=F32)


def band(x, lo, hi):
    lane = lanes(x.shape[0])
    return jnp.where((lane >= lo) & (lane < hi), x, 0.0)


def eye_at(at):
    row = lax.broadcasted_iota(jnp.int32, (W, L), 0)
    return jnp.where(lanes(W) == row + at, jnp.where(row < C, 1.0, 0.0), 0.0)


def unfold(load, store, rows):
    lane = lanes(rows)
    for group in range(5):
        parts = [load(5 * group + q) for q in range(5)]
        for r in range(8):
            q, off = divmod(W * r, L)
            piece = roll(parts[q], -off)
            if off + W > L:
                piece = jnp.where(lane < L - off, piece, roll(parts[q + 1], -off))
            store(8 * group + r, piece)


def kernel(
    res_in, fwd_in, piv_in, bwd_in, flux_in, mass_in, freq_in, order_in,
    upd_out, res_out,
    res, fwd, piv, bwd, flux, mass, freq, order, load_sem,
    placing, moved, spread, tops, xtops, fd, bn, fx, qh, rp, dp, cp,
    st, zz, yl, ym, upd, ph,
    stx, rtx, sux, rux, sty, rty, suy, ruy, swz, rwz, syz, ryz, yloc, cw, pick,
    sl, sh, hl, hh, hs, hn, nh, se, re,
    out_tx, in_tx, out_ux, in_ux, out_ty, in_ty, out_uy, in_uy,
    out_wz, in_wz, out_yz, in_yz, out_h, in_h, out_e, in_e, send_l, recv_l, send_h, recv_h,
):
    patch = lax.axis_index("patch")
    line = lax.axis_index("line")
    patches = lax.axis_size("patch")
    my_y, my_x = line // SIDE, line % SIDE
    before = lax.rem(patch + patches - 1, patches)
    after = lax.rem(patch + 1, patches)

    def in_row(d):
        return lax.rem(my_x + d, SIDE)

    def in_column(d):
        return lax.rem(my_y + d, SIDE)

    def row_peer(d):
        return (patch, my_y * SIDE + in_row(d))

    def column_peer(d):
        return (patch, in_column(d) * SIDE + my_x)

    barrier = pltpu.get_barrier_semaphore()
    for d in range(1, SIDE):
        pl.semaphore_signal(barrier, inc=1, device_id=row_peer(d), device_id_type=MESH)
        pl.semaphore_signal(barrier, inc=1, device_id=column_peer(d), device_id_type=MESH)
    pl.semaphore_signal(barrier, inc=1, device_id=(before, line), device_id_type=MESH)
    pl.semaphore_signal(barrier, inc=1, device_id=(after, line), device_id_type=MESH)

    half_map = C * W
    loads = [
        pltpu.make_async_copy(a, b, load_sem.at[i])
        for i, (a, b) in enumerate((
            (fwd_in.at[0, :, 0:half_map], fwd),
            (order_in, order),
            (res_in, res),
            (piv_in.at[0, :, 0:half_map], piv),
            (bwd_in.at[0, :, 0:half_map], bwd),
            (mass_in, mass),
            (freq_in, freq),
            (flux_in.at[0, :, :, 0:half_map], flux),
        ))
    ]
    for copy in loads:
        copy.start()

    sent = []

    def send(src, dst, out_sem, in_sem, to):
        copy = pltpu.make_async_remote_copy(
            src_ref=src, dst_ref=dst, send_sem=out_sem, recv_sem=in_sem,
            device_id=to, device_id_type=MESH,
        )
        copy.start()
        return copy

    lane = lanes(W)

    wide = lax.broadcasted_iota(jnp.int32, (1, 256), 1)
    for i in range(2):
        cell, slot = wide % L, 32 * (2 * i + wide // L)
        for part, at in ((0, jnp.where(cell < SX, slot + cell, -1)), (1, jnp.where(cell >= L - SX, slot + cell - 96, -1))):
            hit = jnp.where(lax.broadcasted_iota(jnp.int32, (L, 256), 0) == at, 1.0, 0.0).astype(BF16)
            placing[0, i, 2 * L * part : 2 * L * part + L, :] = hit
            placing[0, i, 2 * L * part + L : 2 * L * (part + 1), :] = hit

    tall = lax.broadcasted_iota(jnp.int32, (L, L), 0)
    for part, by in enumerate((-SX, SX)):
        hit = jnp.where(tall == lanes(L) + by, 1.0, 0.0).astype(BF16)
        moved[2 * L * part : 2 * L * part + L, :] = hit
        moved[2 * L * part + L : 2 * L * (part + 1), :] = hit

    wide = lax.broadcasted_iota(jnp.int32, (1, 512), 1)
    place = wide % 256
    group = place // W
    value = place - W * group
    swapped = jnp.where(value < C, value + C, value - C)
    source = jnp.where(wide >= 256, swapped, value) + jnp.where(group == 2, L, 0)
    source = jnp.where(group == 3, -1, source)
    sign = jnp.where(wide >= 256, jnp.where(value < C, -1.0, 1.0), 1.0)
    spread[...] = jnp.where(
        lax.broadcasted_iota(jnp.int32, (256, 512), 0) == source, sign, 0.0
    ).astype(BF16)

    def unfold_map(ref, which):
        def load(q):
            return ref[:, L * q : L * (q + 1)]

        def store(i, piece):
            tops[which, pl.ds(i, K, stride=C), :] = piece

        unfold(load, store, K)

    loads[0].wait()
    unfold_map(fwd, 0)
    loads[1].wait()

    place = lax.broadcasted_iota(jnp.int32, (L, L), 0)
    hot = jnp.where(order[...] == place, 1.0, 0.0).astype(BF16)
    same = jnp.where(lanes(L) == place, 1.0, 0.0).astype(BF16)
    turned_hot = lax.dot_general(same, hot, (((1,), (1,)), ((), ())), preferred_element_type=F32).astype(BF16)
    to_cells = jnp.concatenate([turned_hot, turned_hot], axis=0)
    to_lines = jnp.concatenate([hot, hot], axis=0)

    def pair(x):
        return jnp.concatenate(two(x), axis=1)

    def grid(x):
        return mm(pair(x), to_cells)

    def stored(x):
        return mm(pair(x), to_lines)

    def top_of(which, k):
        return whole_map(tops[which, k * C : (k + 1) * C, :])

    def to_grid(k):
        r = grid(jnp.concatenate([res[k, pl.ds(f, W, stride=2), :] for f in range(2)], axis=0))
        st[k] = jnp.concatenate([r[:W], r[W:]], axis=1)

    def packed(which, k0, count):
        top = tops[which, k0 * C : (k0 + count) * C, :]
        top = jnp.where(lanes(count * C) < W, top, 0.0)
        r = mm(jnp.concatenate(two(top), axis=1), spread[...])
        for k in range(count):
            at = slice(C * k, C * (k + 1))
            yield k0 + k, jnp.concatenate([r[at, :256], r[at, 256:]], axis=0)

    def pack_down():
        for k, block in packed(0, 0, K):
            fd[k, 0:W, :] = block.astype(BF16)
        for k, block in packed(1, 0, K):
            fd[k + 1, W : 2 * W, :] = block.astype(BF16)

    def pack_up():
        for k, block in packed(2, 0, K):
            bn[k] = (-block).astype(BF16)

    loads[2].wait()
    loads[3].wait()
    unfold_map(piv, 1)
    loads[4].wait()
    unfold_map(bwd, 2)
    pack_down()
    to_grid(0)
    to_grid(1)

    def unfold_flux(k, carry):
        def load(q):
            return flux[k, :, L * q : L * (q + 1)]

        def store(i, piece):
            xtops[pl.ds(i, 4, stride=C), :] = piece

        unfold(load, store, 4)
        for d in range(4):
            fx[k, d * W : (d + 1) * W, :] = lhs_of(whole_map(xtops[d * C : (d + 1) * C, :]))
        return carry

    def pack_back(k, carry):
        tile = ym[k]
        at = pl.ds(pl.multiple_of(k * W, W), W)
        qh[0, at, :] = lhs_of(real_form(tile, 80))
        qh[1, at, :] = lhs_of(real_form(tile, 40))
        hs[k] = jnp.where(lanes(C) < W, tile[:C], roll(tile[C:], 48))
        return carry

    def pack_beside(k, carry):
        at = pl.ds(pl.multiple_of(k * W, W), W)
        for side in range(2):
            part = hn[side, k]
            nh[side, at, :] = lhs_of(real_form(jnp.concatenate([part, roll(part, -48)], axis=0), 40))
        return carry

    def step_down(k, x):
        r = mm(fd[k], rhs_of(x))
        zz[k - 1, :, 0 : x.shape[1]] = r[W:]
        new = r[:W, 0:256] + st[k]
        if x.shape[1] > 256:
            new = jnp.concatenate([new, r[:W, 256:]], axis=1)
        return new

    def local_back(x):
        first = x.shape[1] > 256
        end = mm(fd[K, W : 2 * W, :], rhs_of(x))
        if first:
            end_map = end[:, 256:] + band(roll(-top_of(2, K - 1), 40), 40, 80)
            ym[K - 1] = end_map
            end = jnp.concatenate([end[:, :256], end_map], axis=1)
        yl[K - 1] = end[:, :256]
        y = end
        for k in range(K - 2, -1, -1):
            y = mm(bn[k], rhs_of(y)) + zz[k, :, 0 : x.shape[1]]
            yl[k] = y[:, :256]
            if first:
                ym[k] = y[:, 256:]
        if first:
            return y, roll(x[:, 256:], 48) + y[:, 256:]
        return y, None

    def fold_low(x):
        return jnp.where(lanes(C) < 64, x[:C], roll(x[C:], 64))

    def fold_high(x):
        return jnp.where(lanes(C) < 64, roll(x[:C], 64), x[C:])

    def unfold_low(x):
        return jnp.concatenate([x, roll(x, 64)], axis=0)

    def join(x, extra):
        return x if extra is None else jnp.concatenate([x, extra], axis=1)

    def pack_row(j, carry):
        at = pl.ds(pl.multiple_of(j * W, W), W)
        tile = cw[j]
        dp[0, at, :] = lhs_of(real_form(tile, 80))
        dp[1, at, :] = lhs_of(real_form(cw[j + SIDE], 80))
        dp[2, at, :] = lhs_of(real_form(tile, 40))
        return carry

    def to_row(src, dst, three, out_sem, in_sem):
        for d in (2, 1, 3):
            send(src(in_row(d)), dst(my_x), out_sem, in_sem, row_peer(d))
        dst(my_x)[...] = src(my_x)[...]
        sent.append((three, out_sem))
        return three, in_sem

    def to_column(src, dst, three, out_sem, in_sem):
        for d in (2, 1, 3):
            send(src, dst(my_y), out_sem, in_sem, column_peer(d))
        dst(my_y)[...] = src[...]
        sent.append((three, out_sem))
        return three, in_sem

    def bytes_of(ref, sem):
        pltpu.make_async_copy(ref, ref, sem).wait()

    def arrived(copies):
        bytes_of(*copies)

    def edges(pieces):
        low = high = None
        for i, tile in enumerate(pieces):
            a, b = roll(tile, 32 * i), roll(tile, 32 * (i + 1))
            low = a if i == 0 else jnp.where(lane >= 32 * i, a, low)
            high = b if i == 0 else jnp.where(lane >= 32 * i, b, high)
        return low, high

    column = lax.rem(lane, SX)
    half = lane < 64

    for s in range(2):
        first = s == 0
        if first:
            x = jnp.concatenate([st[0], band(roll(top_of(0, 0), 80), 80, 120)], axis=1)
            for k in range(1, K):
                x = step_down(k, x)
                if k + 1 < K:
                    to_grid(k + 1)
                if k == 3:
                    pack_up()
            pl.semaphore_wait(barrier, 8)
        for f in range(2):
            t = x[:, L * f : L * (f + 1)]
            stx[s, 2 * f, 0:C, :] = fold_low(t)
            stx[s, 2 * f + 1, 0:C, :] = fold_high(t)
        if first:
            fold = fold_low(roll(x[:, 256:], 48))
            for j in range(SIDE):
                stx[s, j, C:W, :] = fold
        rows = W if first else C
        t_copies = to_row(
            lambda j: stx.at[s, j, 0:rows], lambda j: rtx.at[s, j, 0:rows],
            rtx.at[s, 0:3, 0:rows], out_tx.at[s], in_tx.at[s]
        )

        y, maps = local_back(x)
        for f in range(2):
            u = y[:, L * f : L * (f + 1)]
            sux[s, 2 * f, 0:C, :] = fold_low(u)
            sux[s, 2 * f + 1, 0:C, :] = fold_high(u)
        if first:
            for j in range(SIDE):
                sux[s, j, C:, :] = maps
        back_rows = W + C if first else C
        u_copies = to_row(
            lambda j: sux.at[s, j, 0:back_rows], lambda j: rux.at[s, j, 0:back_rows],
            rux.at[s, 0:3, 0:back_rows], out_ux.at[s], in_ux.at[s]
        )
        if first:
            lax.fori_loop(0, K, pack_back, 0)
            beside = [
                send(hs, hn.at[0], out_h.at[0], in_h.at[0], (after, line)),
                send(hs, hn.at[1], out_h.at[1], in_h.at[1], (before, line)),
            ]
            sent.append((hs, out_h.at[0]))
            sent.append((hs, out_h.at[1]))
            loads[5].wait()
            loads[6].wait()
            cells_mass = grid(mass[...])
            for f in range(2):
                ph[:, L * f : L * (f + 1)] = freq[f] * cells_mass

        if not first:
            for i in range(2):
                for f in range(2):
                    at = slice(L * f, L * (f + 1))
                    placing[1, i, :, at] = mm(placing[0, i, :, at], to_lines[:L]).astype(BF16)

        arrived(t_copies)
        t = [unfold_low(rtx[s, j, 0:C, :]) for j in range(SIDE)]
        w, wm, w_rhs, q, qm = [None, t[0]], [None] * 5, [None], [None], [None] * SIDE
        if first:
            m = [unfold_low(rtx[s, j, C:W, :]) for j in range(SIDE)]
            for j in range(1, SIDE):
                rp[j, 0:W, :] = lhs_of(real_form(m[j], 0))
            wm[0:2] = [eye_at(80), band(roll(m[0], 80), 80, 120)]
        for j in range(1, SIDE):
            w_rhs.append(rhs_of(join(w[j], wm[j])))
            r = mm(rp[j, 0 : W if first else 2 * W, :], w_rhs[j])
            w.append(r[:W, :L] + t[j])
            if first:
                wm[j + 1] = r[:, L:]
            else:
                q.append(r[W:])
        sty[s, 0:C, :] = fold_low(w[4])
        if first:
            sty[s, C:W, :] = fold_low(roll(wm[4], 48))
        t_copies = to_column(
            sty.at[s, 0:rows], lambda j: rty.at[s, j, 0:rows],
            rty.at[s, 0:3, 0:rows], out_ty.at[s], in_ty.at[s]
        )

        arrived(u_copies)
        u = [unfold_low(rux[s, j, 0:C, :]) for j in range(SIDE)]
        v, vm = [None] * SIDE, [None] * SIDE
        cur_map = None
        if first:
            nq = [rux[s, j, C:, :] for j in range(SIDE)]
            qm[0] = band(nq[0], 80, 120)
            for j in range(1, SIDE):
                rp[j, W : 2 * W, :] = lhs_of(real_form(nq[j], 80))
                r = mm(rp[j, W : 2 * W, :], w_rhs[j])
                q.append(r[:, :L])
                qm[j] = r[:, L:]
            for j in range(SIDE - 1):
                rp[j, 2 * W :, :] = lhs_of(real_form(nq[j], 40))
            vm[3] = eye_at(40)
            cur_map = band(nq[3], 40, 80) + qm[3]
        cur = u[3] + q[3]
        for j in (2, 1, 0):
            v[j], vm[j] = cur, cur_map
            r = mm(rp[j, 2 * W :, :], rhs_of(join(cur, cur_map)))
            cur = r[:, :L] + u[j]
            if j:
                cur = cur + q[j]
            if first:
                cur_map = r[:, L:] + qm[j]
        suy[s, 0:C, :] = fold_low(cur)
        if first:
            suy[s, C:, :] = cur_map
        u_copies = to_column(
            suy.at[s, 0:back_rows], lambda j: ruy.at[s, j, 0:back_rows],
            ruy.at[s, 0:3, 0:back_rows], out_uy.at[s], in_uy.at[s]
        )
        if first:
            for j in range(SIDE):
                cw[j] = wm[j] + band(vm[j], 40, 80)
                cw[j + SIDE] = vm[j]
            lax.fori_loop(0, SIDE, pack_row, 0)
            loads[7].wait()
            lax.fori_loop(0, K // 2, unfold_flux, 0)
        else:
            for copy in beside:
                copy.wait_recv()
            lax.fori_loop(0, K, pack_beside, 0)
        w_own, v_own = w, v

        arrived(t_copies)
        t = [unfold_low(rty[s, j, 0:C, :]) for j in range(SIDE)]
        if first:
            for j in (1, 2):
                cp[j, 0:W, :] = lhs_of(real_form(unfold_low(rty[s, j, C:W, :]), 0))
        w, w_rhs, q = [jnp.zeros((W, L), F32), t[0]], [None], [None]
        for j in (1, 2):
            w_rhs.append(rhs_of(w[j]))
            r = mm(cp[j, 0 : W if first else 2 * W, :], w_rhs[j])
            w.append(r[:W] + t[j])
            if not first:
                q.append(r[W:])
        w_rhs.append(rhs_of(w[3]))
        for j in range(SIDE):
            pick[j] = w[j]
        entry = rhs_of(pick[my_y])
        r = mm(dp[0], entry)
        for j in range(SIDE):
            into = r[W * j : W * (j + 1)]
            swz[s, j] = fold_low(into + w_own[j] if j else into)
        t_copies = to_row(lambda j: swz.at[s, j], lambda j: rwz.at[s, j], rwz.at[s, 0:3], out_wz.at[s], in_wz.at[s])
        r = mm(dp[1], entry)
        for j in range(SIDE):
            into = r[W * j : W * (j + 1)]
            yloc[j] = into + v_own[j] if j < 3 else into
        if not first:
            q.append(mm(cp[3, W : 2 * W, :], w_rhs[3]))

        arrived(u_copies)
        u = [unfold_low(ruy[s, j, 0:C, :]) for j in range(SIDE)]
        if first:
            nq = [ruy[s, j, C:, :] for j in range(SIDE)]
            for j in range(1, SIDE):
                cp[j, W : 2 * W, :] = lhs_of(real_form(nq[j], 80))
                q.append(mm(cp[j, W : 2 * W, :], w_rhs[j]))
            for j in (1, 2):
                cp[j, 2 * W :, :] = lhs_of(real_form(nq[j], 40))
        pick[3] = jnp.zeros((W, L), F32)
        cur = u[3] + q[3]
        for j in (2, 1):
            pick[j] = cur
            cur = mm(cp[j, 2 * W :, :], rhs_of(cur)) + u[j] + q[j]
        pick[0] = cur
        r = mm(dp[2], rhs_of(pick[my_y]))
        for j in range(SIDE):
            syz[s, j] = fold_low(r[W * j : W * (j + 1)] + yloc[j])
        u_copies = to_row(lambda j: syz.at[s, j], lambda j: ryz.at[s, j], ryz.at[s, 0:3], out_yz.at[s], in_yz.at[s])
        if first:
            lax.fori_loop(K // 2, K, unfold_flux, 0)

        def assemble(ref):
            tiles = []
            for f in range(2):
                a, b = ref[s, 2 * f], ref[s, 2 * f + 1]
                tiles.append(
                    jnp.concatenate(
                        [jnp.where(lanes(C) < 64, a, roll(b, 64)), jnp.where(lanes(C) < 64, roll(a, 64), b)], axis=0
                    )
                )
            return jnp.concatenate(tiles, axis=1)

        arrived(t_copies)
        incoming = rhs_of(assemble(rwz))
        def of_block(which, m, x):
            return mm(qh[which, 2 * W * m : 2 * W * (m + 1), :], x)

        low_copies, high_copies, e_copies = [], [], []

        def add_block(which, m, r):
            tiles = []
            for i in range(2):
                k = 2 * m + i
                y = yl[k] + r[W * i : W * (i + 1)]
                yl[k] = y
                if which:
                    upd[k] = RELAXATION * y if first else upd[k] + RELAXATION * y
                tiles += [y[:, :L], y[:, L:]]
            return tiles

        def blocks(which, x, edges_too):
            following = of_block(which, 0, x)
            for m in range(4):
                r, following = following, of_block(which, m + 1, x) if m < 3 else None
                tiles = add_block(which, m, r)
                if edges_too:
                    sl[s, m], sh[s, m] = edges(tiles)
                    high_copies.append(send(sl.at[s, m], hh.at[s, m], send_l.at[s], recv_l.at[s, m], (before, line)))
                    low_copies.append(send(sh.at[s, m], hl.at[s, m], send_h.at[s], recv_h.at[s, m], (after, line)))

        blocks(0, incoming, not first)
        arrived(u_copies)
        a = assemble(ryz)
        if not first:
            se[0] = fold_low(jnp.where(lane < SX, a[:, :L], roll(a[:, L:], SX)))
            se[1] = fold_low(jnp.where(lane < SX, roll(a[:, :L], SX), roll(a[:, L:], 2 * SX)))
            e_copies = [
                send(se.at[1], re.at[0], out_e.at[1], in_e.at[0], (after, line)),
                send(se.at[0], re.at[1], out_e.at[0], in_e.at[1], (before, line)),
            ]
            for side in range(2):
                sent.append((se.at[side], out_e.at[side]))
        blocks(1, rhs_of(a), first)
        sent.append((sl.at[s], send_l.at[s]))
        sent.append((sh.at[s], send_h.at[s]))

        def inner(m, carry):
            ys = [yl[2 * m + i] for i in range(2)]
            rs = [mm(fx[2 * m + i], rhs_of(ys[i])) for i in range(2)]
            for i in range(2):
                k, y, r = 2 * m + i, ys[i], rs[i]
                rows = [
                    jnp.concatenate([*two(r[2 * W : 3 * W, at]), *two(r[3 * W :, at])], axis=1)
                    for at in (slice(0, L), slice(L, 2 * L))
                ]
                spanwise = mm(jnp.concatenate(rows, axis=0), moved[...])
                parts = []
                for f in range(2):
                    at = slice(L * f, L * (f + 1))
                    acc = jnp.where(column > 0, roll(r[0:W, at], 1), 0.0)
                    acc = acc + jnp.where(column < SX - 1, roll(r[W : 2 * W, at], -1), 0.0)
                    parts.append(acc + spanwise[W * f : W * (f + 1)])
                turned = jnp.concatenate([-y[C:], y[:C]], axis=0)
                acc = jnp.concatenate(parts, axis=1) + ph[pl.ds(k, 1), :] * turned
                new = KEEP * st[k] - RELAXATION * acc
                if first:
                    st[k] = new
                else:
                    put(k, upd[k], new)
            return carry

        def put(k, a, b):
            r = stored(jnp.concatenate([a[:, :L], a[:, L:], b[:, :L], b[:, L:]], axis=0))
            for f in range(2):
                upd_out[k, pl.ds(f, W, stride=2), :] = r[W * f : W * (f + 1)]
                res_out[k, pl.ds(f, W, stride=2), :] = r[W * (f + 2) : W * (f + 3)]

        lax.fori_loop(0, 3 if first else 4, inner, 0)

        extra = []
        if not first:
            for copy in (*low_copies, *high_copies, *e_copies):
                copy.wait_recv()
            for side in range(2):
                e = unfold_low(re[side])
                extra.append(mm(nh[side], rhs_of(jnp.where(half, e, roll(e, 64)))))

        def across(m):
            k0, k1 = 2 * m, 2 * m + 1
            sides = [hl[s, m], hh[s, m]]
            if extra:
                sides = [
                    a + jnp.where(half, x[W * k0 : W * k1], x[W * k1 : W * (k1 + 1)]) for a, x in zip(sides, extra)
                ]
            low = jnp.concatenate([fx[k0, 2 * W : 3 * W, :], fx[k1, 2 * W : 3 * W, :]], axis=0)
            high = jnp.concatenate([fx[k0, 3 * W :, :], fx[k1, 3 * W :, :]], axis=0)
            return mm(low, rhs_of(sides[0])), mm(high, rhs_of(sides[1]))

        def placed(products, i):
            at = slice(W * i, W * (i + 1))
            edge = jnp.concatenate([*two(products[0][at]), *two(products[1][at])], axis=1)
            return RELAXATION * mm(edge, placing[s, i])

        def wait_for(m):
            if first:
                low_copies[m].wait_recv()
                high_copies[m].wait_recv()

        wait_for(0)
        following = across(0)
        if first:
            inner(3, 0)
        for m in range(4):
            products, following = following, None
            if m < 3:
                wait_for(m + 1)
                following = across(m + 1)
            for i in range(2):
                k, part = 2 * m + i, placed(products, i)
                if first:
                    current = st[k] - part
                    st[k] = current
                    x = step_down(k, x) if k else current
                else:
                    for f in range(2):
                        rows = pl.ds(f, W, stride=2)
                        res_out[k, rows, :] = res_out[k, rows, :] - part[:, L * f : L * (f + 1)]

    for ref, sem in sent:
        bytes_of(ref, sem)


def shards(residual, forward_maps, pivot_inverse, backward_maps, face_flux, mass_scale, frequencies, line_order):
    vmem = pl.BlockSpec(memory_space=pltpu.VMEM)
    anywhere = pl.BlockSpec(memory_space=pl.ANY)
    dma = pltpu.SemaphoreType.DMA
    out = pltpu.VMEM((K, 2 * W, L), F32)
    update, left = pl.pallas_call(
        kernel,
        out_shape=(out, out),
        in_specs=[anywhere] * 8,
        out_specs=(vmem, vmem),
        scratch_shapes=[
            pltpu.VMEM((K, 2 * W, L), F32),
            pltpu.VMEM((K, C * W), F32),
            pltpu.VMEM((K, C * W), F32),
            pltpu.VMEM((K, C * W), F32),
            pltpu.VMEM((K, 4, C * W), F32),
            pltpu.VMEM((K, L), F32),
            pltpu.SMEM((2,), F32),
            pltpu.VMEM((1, L), jnp.int32),
            dma((8,)),
            pltpu.VMEM((2, 2, 512, 256), BF16),
            pltpu.VMEM((512, L), BF16),
            pltpu.VMEM((256, 512), BF16),
            pltpu.VMEM((3, K * C, L), F32),
            pltpu.VMEM((4 * C, L), F32),
            pltpu.VMEM((K + 1, 2 * W, 256), BF16),
            pltpu.VMEM((K, W, 256), BF16),
            pltpu.VMEM((K, 4 * W, 256), BF16),
            pltpu.VMEM((2, K * W, 256), BF16),
            pltpu.VMEM((SIDE, 3 * W, 256), BF16),
            pltpu.VMEM((3, SIDE * W, 256), BF16),
            pltpu.VMEM((SIDE, 3 * W, 256), BF16),
            pltpu.VMEM((K, W, 256), F32),
            pltpu.VMEM((K, W, 384), F32),
            pltpu.VMEM((K, W, 256), F32),
            pltpu.VMEM((K, W, L), F32),
            pltpu.VMEM((K, W, 256), F32),
            pltpu.VMEM((K, 256), F32),
            pltpu.VMEM((2, SIDE, W, L), F32), pltpu.VMEM((2, SIDE, W, L), F32),
            pltpu.VMEM((2, SIDE, W + C, L), F32), pltpu.VMEM((2, SIDE, W + C, L), F32),
            pltpu.VMEM((2, W, L), F32), pltpu.VMEM((2, SIDE, W, L), F32),
            pltpu.VMEM((2, W + C, L), F32), pltpu.VMEM((2, SIDE, W + C, L), F32),
            pltpu.VMEM((2, SIDE, C, L), F32), pltpu.VMEM((2, SIDE, C, L), F32),
            pltpu.VMEM((2, SIDE, C, L), F32), pltpu.VMEM((2, SIDE, C, L), F32),
            pltpu.VMEM((SIDE, W, L), F32),
            pltpu.VMEM((2 * SIDE, W, L), F32), pltpu.VMEM((SIDE, W, L), F32),
            pltpu.VMEM((2, 4, W, L), F32),
            pltpu.VMEM((2, 4, W, L), F32),
            pltpu.VMEM((2, 4, W, L), F32),
            pltpu.VMEM((2, 4, W, L), F32),
            pltpu.VMEM((K, C, L), F32), pltpu.VMEM((2, K, C, L), F32),
            pltpu.VMEM((2, K * W, 256), BF16),
            pltpu.VMEM((2, C, L), F32), pltpu.VMEM((2, C, L), F32),
            *[dma((2,)) for _ in range(14)],
            dma((2,)), dma((2,)),
            dma((2,)), dma((2, 4)), dma((2,)), dma((2, 4)),
        ],
        compiler_params=pltpu.CompilerParams(collective_id=0, has_side_effects=True),
        name="sweeps",
    )(
        residual.reshape(K, 2 * W, L), forward_maps, pivot_inverse, backward_maps, face_flux,
        mass_scale, frequencies, line_order.reshape(1, L),
    )
    return update.reshape(K, W, 2, L), left.reshape(K, W, 2, L)


def solution(mesh):
    maps = P("patch", "line", None)
    state = P("line", None, None, "patch")
    placed = (state, maps, maps, maps, P("patch", "line", None, None), P("line", "patch"), P(), P("patch"))
    return jax.shard_map(
        shards, mesh=mesh, in_specs=placed, out_specs=(state, state), check_vma=False
    )
```

```python
import functools

import jax
import jax.numpy as jnp
from jax import lax
from jax.experimental import pallas as pl
from jax.experimental.pallas import tpu as pltpu
from jax.sharding import PartitionSpec as P

SX = 32
RELAXATION = 0.8
KEEP = 1.0 - RELAXATION
C = 40
W = 80
K = 8
L = 128
SIDE = 4
F32 = jnp.float32
BF16 = jnp.bfloat16
MESH = pl.DeviceIdType.MESH


def lanes(rows, width=L):
    return lax.broadcasted_iota(jnp.int32, (rows, width), 1)


def roll(x, by):
    by = by % L
    return x if by == 0 else pltpu.roll(x, by, 1)


def two(x):
    high = x.astype(BF16)
    return high, (x - high.astype(F32)).astype(BF16)


def rhs_of(x):
    high, low = two(x)
    return jnp.concatenate([high, low, high, jnp.zeros((16, x.shape[1]), BF16)], axis=0)


def lhs_of(w):
    lane = lanes(w.shape[0])
    high = w.astype(BF16).astype(F32)
    low = w - high
    moved = roll(high, W)
    first = jnp.where(lane < W, high, moved)
    second = jnp.where(lane < 32, moved, roll(low, 32))
    return jnp.concatenate([first, second], axis=1).astype(BF16)


def real_form(tile, at):
    lane = lanes(W)
    plain = roll(tile, -at)
    moved = roll(tile, C - at)
    turned = jnp.concatenate([-moved[C:], moved[:C]], axis=0)
    return jnp.where(lane < C, plain, jnp.where(lane < W, turned, 0.0))


def whole_map(top):
    lane = lanes(C)
    top = jnp.where(lane < W, top, 0.0)
    bottom = jnp.where(lane < C, -roll(top, -C), jnp.where(lane < W, roll(top, C), 0.0))
    return jnp.concatenate([top, bottom], axis=0)


def mm(a, b):
    return jnp.dot(a, b, preferred_element_type=F32)


def band(x, lo, hi):
    lane = lanes(x.shape[0])
    return jnp.where((lane >= lo) & (lane < hi), x, 0.0)


def eye_at(at):
    row = lax.broadcasted_iota(jnp.int32, (W, L), 0)
    return jnp.where(lanes(W) == row + at, jnp.where(row < C, 1.0, 0.0), 0.0)


def unfold(load, store, rows):
    lane = lanes(rows)
    for group in range(5):
        parts = [load(5 * group + q) for q in range(5)]
        for r in range(8):
            q, off = divmod(W * r, L)
            piece = roll(parts[q], -off)
            if off + W > L:
                piece = jnp.where(lane < L - off, piece, roll(parts[q + 1], -off))
            store(8 * group + r, piece)


def kernel(
    res_in, fwd_in, piv_in, bwd_in, flux_in, mass_in, freq_in, order_in,
    upd_out, res_out,
    res, fwd, piv, bwd, flux, mass, freq, order, load_sem,
    placing, moved, spread, tops, xtops, fd, bn, fx, qh, rp, dp, cp,
    st, zz, yl, ym, upd, ph,
    stx, rtx, sux, rux, sty, rty, suy, ruy, swz, rwz, syz, ryz, yloc, cw, pick,
    sl, sh, hl, hh, hs, hn, nh, se, re,
    out_tx, in_tx, out_ux, in_ux, out_ty, in_ty, out_uy, in_uy,
    out_wz, in_wz, out_yz, in_yz, out_h, in_h, out_e, in_e, send_l, recv_l, send_h, recv_h,
):
    patch = lax.axis_index("patch")
    line = lax.axis_index("line")
    patches = lax.axis_size("patch")
    my_y, my_x = line // SIDE, line % SIDE
    before = lax.rem(patch + patches - 1, patches)
    after = lax.rem(patch + 1, patches)

    def in_row(d):
        return lax.rem(my_x + d, SIDE)

    def in_column(d):
        return lax.rem(my_y + d, SIDE)

    def row_peer(d):
        return (patch, my_y * SIDE + in_row(d))

    def column_peer(d):
        return (patch, in_column(d) * SIDE + my_x)

    barrier = pltpu.get_barrier_semaphore()
    for d in range(1, SIDE):
        pl.semaphore_signal(barrier, inc=1, device_id=row_peer(d), device_id_type=MESH)
        pl.semaphore_signal(barrier, inc=1, device_id=column_peer(d), device_id_type=MESH)
    pl.semaphore_signal(barrier, inc=1, device_id=(before, line), device_id_type=MESH)
    pl.semaphore_signal(barrier, inc=1, device_id=(after, line), device_id_type=MESH)

    half_map = C * W
    loads = [
        pltpu.make_async_copy(a, b, load_sem.at[i])
        for i, (a, b) in enumerate((
            (fwd_in.at[0, :, 0:half_map], fwd),
            (order_in, order),
            (res_in, res),
            (piv_in.at[0, :, 0:half_map], piv),
            (bwd_in.at[0, :, 0:half_map], bwd),
            (mass_in, mass),
            (freq_in, freq),
            (flux_in.at[0, :, :, 0:half_map], flux),
        ))
    ]
    for copy in loads:
        copy.start()

    sent = []

    def send(src, dst, out_sem, in_sem, to):
        copy = pltpu.make_async_remote_copy(
            src_ref=src, dst_ref=dst, send_sem=out_sem, recv_sem=in_sem,
            device_id=to, device_id_type=MESH,
        )
        copy.start()
        return copy

    lane = lanes(W)

    wide = lax.broadcasted_iota(jnp.int32, (1, 256), 1)
    for i in range(2):
        cell, slot = wide % L, 32 * (2 * i + wide // L)
        for part, at in ((0, jnp.where(cell < SX, slot + cell, -1)), (1, jnp.where(cell >= L - SX, slot + cell - 96, -1))):
            hit = jnp.where(lax.broadcasted_iota(jnp.int32, (L, 256), 0) == at, 1.0, 0.0).astype(BF16)
            placing[0, i, 2 * L * part : 2 * L * part + L, :] = hit
            placing[0, i, 2 * L * part + L : 2 * L * (part + 1), :] = hit

    tall = lax.broadcasted_iota(jnp.int32, (L, L), 0)
    for part, by in enumerate((-SX, SX)):
        hit = jnp.where(tall == lanes(L) + by, 1.0, 0.0).astype(BF16)
        moved[2 * L * part : 2 * L * part + L, :] = hit
        moved[2 * L * part + L : 2 * L * (part + 1), :] = hit

    wide = lax.broadcasted_iota(jnp.int32, (1, 512), 1)
    place = wide % 256
    group = place // W
    value = place - W * group
    swapped = jnp.where(value < C, value + C, value - C)
    source = jnp.where(wide >= 256, swapped, value) + jnp.where(group == 2, L, 0)
    source = jnp.where(group == 3, -1, source)
    sign = jnp.where(wide >= 256, jnp.where(value < C, -1.0, 1.0), 1.0)
    spread[...] = jnp.where(
        lax.broadcasted_iota(jnp.int32, (256, 512), 0) == source, sign, 0.0
    ).astype(BF16)

    def unfold_map(ref, which):
        def load(q):
            return ref[:, L * q : L * (q + 1)]

        def store(i, piece):
            tops[which, pl.ds(i, K, stride=C), :] = piece

        unfold(load, store, K)

    loads[0].wait()
    unfold_map(fwd, 0)
    loads[1].wait()

    place = lax.broadcasted_iota(jnp.int32, (L, L), 0)
    hot = jnp.where(order[...] == place, 1.0, 0.0).astype(BF16)
    same = jnp.where(lanes(L) == place, 1.0, 0.0).astype(BF16)
    turned_hot = lax.dot_general(same, hot, (((1,), (1,)), ((), ())), preferred_element_type=F32).astype(BF16)
    to_cells = jnp.concatenate([turned_hot, turned_hot], axis=0)
    to_lines = jnp.concatenate([hot, hot], axis=0)

    def pair(x):
        return jnp.concatenate(two(x), axis=1)

    def grid(x):
        return mm(pair(x), to_cells)

    def stored(x):
        return mm(pair(x), to_lines)

    def top_of(which, k):
        return whole_map(tops[which, k * C : (k + 1) * C, :])

    def to_grid(k):
        r = grid(jnp.concatenate([res[k, pl.ds(f, W, stride=2), :] for f in range(2)], axis=0))
        st[k] = jnp.concatenate([r[:W], r[W:]], axis=1)

    def packed(which, k0, count):
        top = tops[which, k0 * C : (k0 + count) * C, :]
        top = jnp.where(lanes(count * C) < W, top, 0.0)
        r = mm(jnp.concatenate(two(top), axis=1), spread[...])
        for k in range(count):
            at = slice(C * k, C * (k + 1))
            yield k0 + k, jnp.concatenate([r[at, :256], r[at, 256:]], axis=0)

    def pack_down():
        for k, block in packed(0, 0, K):
            fd[k, 0:W, :] = block.astype(BF16)
        for k, block in packed(1, 0, K):
            fd[k + 1, W : 2 * W, :] = block.astype(BF16)

    def pack_up():
        for k, block in packed(2, 0, K):
            bn[k] = (-block).astype(BF16)

    loads[2].wait()
    loads[3].wait()
    unfold_map(piv, 1)
    loads[4].wait()
    unfold_map(bwd, 2)
    pack_down()
    to_grid(0)
    to_grid(1)

    def unfold_flux(k, carry):
        def load(q):
            return flux[k, :, L * q : L * (q + 1)]

        def store(i, piece):
            xtops[pl.ds(i, 4, stride=C), :] = piece

        unfold(load, store, 4)
        for d in range(4):
            fx[k, d * W : (d + 1) * W, :] = lhs_of(whole_map(xtops[d * C : (d + 1) * C, :]))
        return carry

    def pack_back(k, carry):
        tile = ym[k]
        at = pl.ds(pl.multiple_of(k * W, W), W)
        qh[0, at, :] = lhs_of(real_form(tile, 80))
        qh[1, at, :] = lhs_of(real_form(tile, 40))
        hs[k] = jnp.where(lanes(C) < W, tile[:C], roll(tile[C:], 48))
        return carry

    def pack_beside(k, carry):
        at = pl.ds(pl.multiple_of(k * W, W), W)
        for side in range(2):
            part = hn[side, k]
            nh[side, at, :] = lhs_of(real_form(jnp.concatenate([part, roll(part, -48)], axis=0), 40))
        return carry

    def step_down(k, x):
        r = mm(fd[k], rhs_of(x))
        zz[k - 1, :, 0 : x.shape[1]] = r[W:]
        new = r[:W, 0:256] + st[k]
        if x.shape[1] > 256:
            new = jnp.concatenate([new, r[:W, 256:]], axis=1)
        return new

    def local_back(x):
        first = x.shape[1] > 256
        end = mm(fd[K, W : 2 * W, :], rhs_of(x))
        if first:
            end_map = end[:, 256:] + band(roll(-top_of(2, K - 1), 40), 40, 80)
            ym[K - 1] = end_map
            end = jnp.concatenate([end[:, :256], end_map], axis=1)
        yl[K - 1] = end[:, :256]
        y = end
        for k in range(K - 2, -1, -1):
            y = mm(bn[k], rhs_of(y)) + zz[k, :, 0 : x.shape[1]]
            yl[k] = y[:, :256]
            if first:
                ym[k] = y[:, 256:]
        if first:
            return y, roll(x[:, 256:], 48) + y[:, 256:]
        return y, None

    def fold_low(x):
        return jnp.where(lanes(C) < 64, x[:C], roll(x[C:], 64))

    def fold_high(x):
        return jnp.where(lanes(C) < 64, roll(x[:C], 64), x[C:])

    def unfold_low(x):
        return jnp.concatenate([x, roll(x, 64)], axis=0)

    def join(x, extra):
        return x if extra is None else jnp.concatenate([x, extra], axis=1)

    def pack_row(j, carry):
        at = pl.ds(pl.multiple_of(j * W, W), W)
        tile = cw[j]
        dp[0, at, :] = lhs_of(real_form(tile, 80))
        dp[1, at, :] = lhs_of(real_form(cw[j + SIDE], 80))
        dp[2, at, :] = lhs_of(real_form(tile, 40))
        return carry

    def to_row(src, dst, three, out_sem, in_sem):
        for d in (2, 1, 3):
            send(src(in_row(d)), dst(my_x), out_sem, in_sem, row_peer(d))
        dst(my_x)[...] = src(my_x)[...]
        sent.append((three, out_sem))
        return three, in_sem

    def to_column(src, dst, three, out_sem, in_sem):
        for d in (2, 1, 3):
            send(src, dst(my_y), out_sem, in_sem, column_peer(d))
        dst(my_y)[...] = src[...]
        sent.append((three, out_sem))
        return three, in_sem

    def bytes_of(ref, sem):
        pltpu.make_async_copy(ref, ref, sem).wait()

    def arrived(copies):
        bytes_of(*copies)

    def edges(pieces):
        low = high = None
        for i, tile in enumerate(pieces):
            a, b = roll(tile, 32 * i), roll(tile, 32 * (i + 1))
            low = a if i == 0 else jnp.where(lane >= 32 * i, a, low)
            high = b if i == 0 else jnp.where(lane >= 32 * i, b, high)
        return low, high

    column = lax.rem(lane, SX)
    half = lane < 64

    for s in range(2):
        first = s == 0
        if first:
            x = jnp.concatenate([st[0], band(roll(top_of(0, 0), 80), 80, 120)], axis=1)
            for k in range(1, K):
                x = step_down(k, x)
                if k + 1 < K:
                    to_grid(k + 1)
                if k == 3:
                    pack_up()
            pl.semaphore_wait(barrier, 8)
        for f in range(2):
            t = x[:, L * f : L * (f + 1)]
            stx[s, 2 * f, 0:C, :] = fold_low(t)
            stx[s, 2 * f + 1, 0:C, :] = fold_high(t)
        if first:
            fold = fold_low(roll(x[:, 256:], 48))
            for j in range(SIDE):
                stx[s, j, C:W, :] = fold
        rows = W if first else C
        t_copies = to_row(
            lambda j: stx.at[s, j, 0:rows], lambda j: rtx.at[s, j, 0:rows],
            rtx.at[s, 0:3, 0:rows], out_tx.at[s], in_tx.at[s]
        )

        y, maps = local_back(x)
        for f in range(2):
            u = y[:, L * f : L * (f + 1)]
            sux[s, 2 * f, 0:C, :] = fold_low(u)
            sux[s, 2 * f + 1, 0:C, :] = fold_high(u)
        if first:
            for j in range(SIDE):
                sux[s, j, C:, :] = maps
        back_rows = W + C if first else C
        u_copies = to_row(
            lambda j: sux.at[s, j, 0:back_rows], lambda j: rux.at[s, j, 0:back_rows],
            rux.at[s, 0:3, 0:back_rows], out_ux.at[s], in_ux.at[s]
        )
        if first:
            lax.fori_loop(0, K, pack_back, 0)
            beside = [
                send(hs, hn.at[0], out_h.at[0], in_h.at[0], (after, line)),
                send(hs, hn.at[1], out_h.at[1], in_h.at[1], (before, line)),
            ]
            sent.append((hs, out_h.at[0]))
            sent.append((hs, out_h.at[1]))
            loads[5].wait()
            loads[6].wait()
            cells_mass = grid(mass[...])
            for f in range(2):
                ph[:, L * f : L * (f + 1)] = freq[f] * cells_mass

        if not first:
            for i in range(2):
                for f in range(2):
                    at = slice(L * f, L * (f + 1))
                    placing[1, i, :, at] = mm(placing[0, i, :, at], to_lines[:L]).astype(BF16)

        arrived(t_copies)
        t = [unfold_low(rtx[s, j, 0:C, :]) for j in range(SIDE)]
        w, wm, w_rhs, q, qm = [None, t[0]], [None] * 5, [None], [None], [None] * SIDE
        if first:
            m = [unfold_low(rtx[s, j, C:W, :]) for j in range(SIDE)]
            for j in range(1, SIDE):
                rp[j, 0:W, :] = lhs_of(real_form(m[j], 0))
            wm[0:2] = [eye_at(80), band(roll(m[0], 80), 80, 120)]
        for j in range(1, SIDE):
            w_rhs.append(rhs_of(join(w[j], wm[j])))
            r = mm(rp[j, 0 : W if first else 2 * W, :], w_rhs[j])
            w.append(r[:W, :L] + t[j])
            if first:
                wm[j + 1] = r[:, L:]
            else:
                q.append(r[W:])
        sty[s, 0:C, :] = fold_low(w[4])
        if first:
            sty[s, C:W, :] = fold_low(roll(wm[4], 48))
        t_copies = to_column(
            sty.at[s, 0:rows], lambda j: rty.at[s, j, 0:rows],
            rty.at[s, 0:3, 0:rows], out_ty.at[s], in_ty.at[s]
        )

        arrived(u_copies)
        u = [unfold_low(rux[s, j, 0:C, :]) for j in range(SIDE)]
        v, vm = [None] * SIDE, [None] * SIDE
        cur_map = None
        if first:
            nq = [rux[s, j, C:, :] for j in range(SIDE)]
            qm[0] = band(nq[0], 80, 120)
            for j in range(1, SIDE):
                rp[j, W : 2 * W, :] = lhs_of(real_form(nq[j], 80))
                r = mm(rp[j, W : 2 * W, :], w_rhs[j])
                q.append(r[:, :L])
                qm[j] = r[:, L:]
            for j in range(SIDE - 1):
                rp[j, 2 * W :, :] = lhs_of(real_form(nq[j], 40))
            vm[3] = eye_at(40)
            cur_map = band(nq[3], 40, 80) + qm[3]
        cur = u[3] + q[3]
        for j in (2, 1, 0):
            v[j], vm[j] = cur, cur_map
            r = mm(rp[j, 2 * W :, :], rhs_of(join(cur, cur_map)))
            cur = r[:, :L] + u[j]
            if j:
                cur = cur + q[j]
            if first:
                cur_map = r[:, L:] + qm[j]
        suy[s, 0:C, :] = fold_low(cur)
        if first:
            suy[s, C:, :] = cur_map
        u_copies = to_column(
            suy.at[s, 0:back_rows], lambda j: ruy.at[s, j, 0:back_rows],
            ruy.at[s, 0:3, 0:back_rows], out_uy.at[s], in_uy.at[s]
        )
        if first:
            for j in range(SIDE):
                cw[j] = wm[j] + band(vm[j], 40, 80)
                cw[j + SIDE] = vm[j]
            lax.fori_loop(0, SIDE, pack_row, 0)
            loads[7].wait()
            lax.fori_loop(0, K // 2, unfold_flux, 0)
        else:
            for copy in beside:
                copy.wait_recv()
            lax.fori_loop(0, K, pack_beside, 0)
        w_own, v_own = w, v

        arrived(t_copies)
        t = [unfold_low(rty[s, j, 0:C, :]) for j in range(SIDE)]
        if first:
            for j in (1, 2):
                cp[j, 0:W, :] = lhs_of(real_form(unfold_low(rty[s, j, C:W, :]), 0))
        w, w_rhs, q = [jnp.zeros((W, L), F32), t[0]], [None], [None]
        for j in (1, 2):
            w_rhs.append(rhs_of(w[j]))
            r = mm(cp[j, 0 : W if first else 2 * W, :], w_rhs[j])
            w.append(r[:W] + t[j])
            if not first:
                q.append(r[W:])
        w_rhs.append(rhs_of(w[3]))
        for j in range(SIDE):
            pick[j] = w[j]
        entry = rhs_of(pick[my_y])
        r = mm(dp[0], entry)
        for j in range(SIDE):
            into = r[W * j : W * (j + 1)]
            swz[s, j] = fold_low(into + w_own[j] if j else into)
        t_copies = to_row(lambda j: swz.at[s, j], lambda j: rwz.at[s, j], rwz.at[s, 0:3], out_wz.at[s], in_wz.at[s])
        r = mm(dp[1], entry)
        for j in range(SIDE):
            into = r[W * j : W * (j + 1)]
            yloc[j] = into + v_own[j] if j < 3 else into
        if not first:
            q.append(mm(cp[3, W : 2 * W, :], w_rhs[3]))

        arrived(u_copies)
        u = [unfold_low(ruy[s, j, 0:C, :]) for j in range(SIDE)]
        if first:
            nq = [ruy[s, j, C:, :] for j in range(SIDE)]
            for j in range(1, SIDE):
                cp[j, W : 2 * W, :] = lhs_of(real_form(nq[j], 80))
                q.append(mm(cp[j, W : 2 * W, :], w_rhs[j]))
            for j in (1, 2):
                cp[j, 2 * W :, :] = lhs_of(real_form(nq[j], 40))
        pick[3] = jnp.zeros((W, L), F32)
        cur = u[3] + q[3]
        for j in (2, 1):
            pick[j] = cur
            cur = mm(cp[j, 2 * W :, :], rhs_of(cur)) + u[j] + q[j]
        pick[0] = cur
        r = mm(dp[2], rhs_of(pick[my_y]))
        for j in range(SIDE):
            syz[s, j] = fold_low(r[W * j : W * (j + 1)] + yloc[j])
        u_copies = to_row(lambda j: syz.at[s, j], lambda j: ryz.at[s, j], ryz.at[s, 0:3], out_yz.at[s], in_yz.at[s])
        if first:
            lax.fori_loop(K // 2, K, unfold_flux, 0)

        def assemble(ref):
            tiles = []
            for f in range(2):
                a, b = ref[s, 2 * f], ref[s, 2 * f + 1]
                tiles.append(
                    jnp.concatenate(
                        [jnp.where(lanes(C) < 64, a, roll(b, 64)), jnp.where(lanes(C) < 64, roll(a, 64), b)], axis=0
                    )
                )
            return jnp.concatenate(tiles, axis=1)

        arrived(t_copies)
        incoming = rhs_of(assemble(rwz))
        def of_block(which, m, x):
            return mm(qh[which, 2 * W * m : 2 * W * (m + 1), :], x)

        low_copies, high_copies, e_copies = [], [], []

        def add_block(which, m, r):
            tiles = []
            for i in range(2):
                k = 2 * m + i
                y = yl[k] + r[W * i : W * (i + 1)]
                yl[k] = y
                if which:
                    upd[k] = RELAXATION * y if first else upd[k] + RELAXATION * y
                tiles += [y[:, :L], y[:, L:]]
            return tiles

        def blocks(which, x, edges_too):
            following = of_block(which, 0, x)
            for m in range(4):
                r, following = following, of_block(which, m + 1, x) if m < 3 else None
                tiles = add_block(which, m, r)
                if edges_too:
                    sl[s, m], sh[s, m] = edges(tiles)
                    high_copies.append(send(sl.at[s, m], hh.at[s, m], send_l.at[s], recv_l.at[s, m], (before, line)))
                    low_copies.append(send(sh.at[s, m], hl.at[s, m], send_h.at[s], recv_h.at[s, m], (after, line)))

        blocks(0, incoming, not first)
        arrived(u_copies)
        a = assemble(ryz)
        if not first:
            se[0] = fold_low(jnp.where(lane < SX, a[:, :L], roll(a[:, L:], SX)))
            se[1] = fold_low(jnp.where(lane < SX, roll(a[:, :L], SX), roll(a[:, L:], 2 * SX)))
            e_copies = [
                send(se.at[1], re.at[0], out_e.at[1], in_e.at[0], (after, line)),
                send(se.at[0], re.at[1], out_e.at[0], in_e.at[1], (before, line)),
            ]
            for side in range(2):
                sent.append((se.at[side], out_e.at[side]))
        blocks(1, rhs_of(a), first)
        sent.append((sl.at[s], send_l.at[s]))
        sent.append((sh.at[s], send_h.at[s]))

        def inner(m, carry):
            ys = [yl[2 * m + i] for i in range(2)]
            rs = [mm(fx[2 * m + i], rhs_of(ys[i])) for i in range(2)]
            for i in range(2):
                k, y, r = 2 * m + i, ys[i], rs[i]
                rows = [
                    jnp.concatenate([*two(r[2 * W : 3 * W, at]), *two(r[3 * W :, at])], axis=1)
                    for at in (slice(0, L), slice(L, 2 * L))
                ]
                spanwise = mm(jnp.concatenate(rows, axis=0), moved[...])
                parts = []
                for f in range(2):
                    at = slice(L * f, L * (f + 1))
                    acc = jnp.where(column > 0, roll(r[0:W, at], 1), 0.0)
                    acc = acc + jnp.where(column < SX - 1, roll(r[W : 2 * W, at], -1), 0.0)
                    parts.append(acc + spanwise[W * f : W * (f + 1)])
                turned = jnp.concatenate([-y[C:], y[:C]], axis=0)
                acc = jnp.concatenate(parts, axis=1) + ph[pl.ds(k, 1), :] * turned
                new = KEEP * st[k] - RELAXATION * acc
                if first:
                    st[k] = new
                else:
                    put(k, upd[k], new)
            return carry

        def put(k, a, b):
            r = stored(jnp.concatenate([a[:, :L], a[:, L:], b[:, :L], b[:, L:]], axis=0))
            for f in range(2):
                upd_out[k, pl.ds(f, W, stride=2), :] = r[W * f : W * (f + 1)]
                res_out[k, pl.ds(f, W, stride=2), :] = r[W * (f + 2) : W * (f + 3)]

        lax.fori_loop(0, 3, inner, 0)

        extra = []
        if not first:
            for copy in (*low_copies, *high_copies, *e_copies):
                copy.wait_recv()
            for side in range(2):
                e = unfold_low(re[side])
                extra.append(mm(nh[side], rhs_of(jnp.where(half, e, roll(e, 64)))))

        def across(m):
            k0, k1 = 2 * m, 2 * m + 1
            sides = [hl[s, m], hh[s, m]]
            if extra:
                sides = [
                    a + jnp.where(half, x[W * k0 : W * k1], x[W * k1 : W * (k1 + 1)]) for a, x in zip(sides, extra)
                ]
            low = jnp.concatenate([fx[k0, 2 * W : 3 * W, :], fx[k1, 2 * W : 3 * W, :]], axis=0)
            high = jnp.concatenate([fx[k0, 3 * W :, :], fx[k1, 3 * W :, :]], axis=0)
            return mm(low, rhs_of(sides[0])), mm(high, rhs_of(sides[1]))

        def placed(products, i):
            at = slice(W * i, W * (i + 1))
            edge = jnp.concatenate([*two(products[0][at]), *two(products[1][at])], axis=1)
            return RELAXATION * mm(edge, placing[s, i])

        def wait_for(m):
            if first:
                low_copies[m].wait_recv()
                high_copies[m].wait_recv()

        wait_for(0)
        following = across(0)
        inner(3, 0)
        for m in range(4):
            products, following = following, None
            if m < 3:
                wait_for(m + 1)
                following = across(m + 1)
            for i in range(2):
                k, part = 2 * m + i, placed(products, i)
                if first:
                    current = st[k] - part
                    st[k] = current
                    x = step_down(k, x) if k else current
                else:
                    for f in range(2):
                        rows = pl.ds(f, W, stride=2)
                        res_out[k, rows, :] = res_out[k, rows, :] - part[:, L * f : L * (f + 1)]

    for ref, sem in sent:
        bytes_of(ref, sem)


def shards(residual, forward_maps, pivot_inverse, backward_maps, face_flux, mass_scale, frequencies, line_order):
    vmem = pl.BlockSpec(memory_space=pltpu.VMEM)
    anywhere = pl.BlockSpec(memory_space=pl.ANY)
    dma = pltpu.SemaphoreType.DMA
    out = pltpu.VMEM((K, 2 * W, L), F32)
    update, left = pl.pallas_call(
        kernel,
        out_shape=(out, out),
        in_specs=[anywhere] * 8,
        out_specs=(vmem, vmem),
        scratch_shapes=[
            pltpu.VMEM((K, 2 * W, L), F32),
            pltpu.VMEM((K, C * W), F32),
            pltpu.VMEM((K, C * W), F32),
            pltpu.VMEM((K, C * W), F32),
            pltpu.VMEM((K, 4, C * W), F32),
            pltpu.VMEM((K, L), F32),
            pltpu.SMEM((2,), F32),
            pltpu.VMEM((1, L), jnp.int32),
            dma((8,)),
            pltpu.VMEM((2, 2, 512, 256), BF16),
            pltpu.VMEM((512, L), BF16),
            pltpu.VMEM((256, 512), BF16),
            pltpu.VMEM((3, K * C, L), F32),
            pltpu.VMEM((4 * C, L), F32),
            pltpu.VMEM((K + 1, 2 * W, 256), BF16),
            pltpu.VMEM((K, W, 256), BF16),
            pltpu.VMEM((K, 4 * W, 256), BF16),
            pltpu.VMEM((2, K * W, 256), BF16),
            pltpu.VMEM((SIDE, 3 * W, 256), BF16),
            pltpu.VMEM((3, SIDE * W, 256), BF16),
            pltpu.VMEM((SIDE, 3 * W, 256), BF16),
            pltpu.VMEM((K, W, 256), F32),
            pltpu.VMEM((K, W, 384), F32),
            pltpu.VMEM((K, W, 256), F32),
            pltpu.VMEM((K, W, L), F32),
            pltpu.VMEM((K, W, 256), F32),
            pltpu.VMEM((K, 256), F32),
            pltpu.VMEM((2, SIDE, W, L), F32), pltpu.VMEM((2, SIDE, W, L), F32),
            pltpu.VMEM((2, SIDE, W + C, L), F32), pltpu.VMEM((2, SIDE, W + C, L), F32),
            pltpu.VMEM((2, W, L), F32), pltpu.VMEM((2, SIDE, W, L), F32),
            pltpu.VMEM((2, W + C, L), F32), pltpu.VMEM((2, SIDE, W + C, L), F32),
            pltpu.VMEM((2, SIDE, C, L), F32), pltpu.VMEM((2, SIDE, C, L), F32),
            pltpu.VMEM((2, SIDE, C, L), F32), pltpu.VMEM((2, SIDE, C, L), F32),
            pltpu.VMEM((SIDE, W, L), F32),
            pltpu.VMEM((2 * SIDE, W, L), F32), pltpu.VMEM((SIDE, W, L), F32),
            pltpu.VMEM((2, 4, W, L), F32),
            pltpu.VMEM((2, 4, W, L), F32),
            pltpu.VMEM((2, 4, W, L), F32),
            pltpu.VMEM((2, 4, W, L), F32),
            pltpu.VMEM((K, C, L), F32), pltpu.VMEM((2, K, C, L), F32),
            pltpu.VMEM((2, K * W, 256), BF16),
            pltpu.VMEM((2, C, L), F32), pltpu.VMEM((2, C, L), F32),
            *[dma((2,)) for _ in range(14)],
            dma((2,)), dma((2,)),
            dma((2,)), dma((2, 4)), dma((2,)), dma((2, 4)),
        ],
        compiler_params=pltpu.CompilerParams(collective_id=0, has_side_effects=True),
        name="sweeps",
    )(
        residual.reshape(K, 2 * W, L), forward_maps, pivot_inverse, backward_maps, face_flux,
        mass_scale, frequencies, line_order.reshape(1, L),
    )
    return update.reshape(K, W, 2, L), left.reshape(K, W, 2, L)


def solution(mesh):
    maps = P("patch", "line", None)
    state = P("line", None, None, "patch")
    placed = (state, maps, maps, maps, P("patch", "line", None, None), P("line", "patch"), P(), P("patch"))
    return jax.shard_map(
        shards, mesh=mesh, in_specs=placed, out_specs=(state, state), check_vma=False
    )
```
